32 devices in a mesh: chan: 8 (over z, x), band: 4 (over y, core).
Axes of the slice: x: 2, y: 2, z: 4, core: 2. Of those that a mesh axis runs over, the one named last changes fastest.
Arguments:
- spectra: bfloat16 [8, 2, 4096, 512], P('band', None, 'chan'), may hold values from -64 to 64
- half_width: int32 [512], replicated, may hold values from 1 to 32, as said below
- panel_block: int32 [4], replicated, may hold values from 0 to 7
- panel_offset: int32 [4], replicated, may hold values from 0 to 256
Outputs:
- cross: bfloat16 [4, 8, 2, 4096, 256], P(None, 'band', None, 'chan')
The draws below stay inside these ranges and needn't reach their ends.
Inputs may be any that keep to these rules, and one draw needn't show every extreme that they name: `half_width`: some window's half-width is exactly 32.
All inputs are finite; a program needn't handle non-finite values.
Results may differ from the reference program's by a relative error of at most 0.0056.
Values may be sent and summed in bfloat16 or wider, within the bound.
No kernel may reach another device: no remote copies, remote signals or barrier semaphores. Data moves between devices by JAX's collectives and lax.ppermute only.
A program may use at most 64 MiB of HBM per device.

```python
import math
import jax
import jax.numpy as jnp
import numpy as np
from jax import lax

CH_DEV = 512
W = 512
PANEL = 256
NPANEL = 4
HALO = 32
CHANNELS = 4096
NF = 8
N_CHAN = 8


def draw_spectra(key, part):
    keys = jax.random.split(jax.random.fold_in(key, 11), 4)
    position = jnp.arange(NF, dtype=jnp.float32) / max(NF - 1, 1)
    bin_amp = 3.0 ** position * jnp.exp(jax.random.uniform(keys[0], (NF,), jnp.float32, jnp.log(0.7), jnp.log(1.4)))
    chan_amp = jnp.exp(jax.random.uniform(keys[1], (CHANNELS,), jnp.float32, jnp.log(0.5), jnp.log(2.0)))
    win_amp = jnp.exp(jax.random.uniform(keys[2], (W,), jnp.float32, jnp.log(0.5), jnp.log(2.0)))
    noise = jnp.clip(jax.random.normal(keys[3], (NF, 2, CHANNELS, W), jnp.float32), -4.0, 4.0)
    values = noise * bin_amp[:, None, None, None] * chan_amp[None, None, :, None] * win_amp[None, None, None, :]
    return jnp.clip(values, -64.0, 64.0).astype(jnp.bfloat16)


def draw_half_width(key, part):
    keys = jax.random.split(jax.random.fold_in(key, 23), 2)
    widths = jax.random.randint(keys[0], (W,), 1, HALO + 1, dtype=jnp.int32)
    where_top = jax.random.randint(keys[1], (), 0, W, dtype=jnp.int32)
    return widths.at[where_top].set(HALO)


def touch_ends(drawn, rng, low, high):
    spot = [jax.random.randint(jax.random.fold_in(rng, axis), (), 0, length) for axis, length in enumerate(drawn.shape)]
    widest = drawn.shape.index(max(drawn.shape))
    neighbour = spot[:widest] + [(spot[widest] + 1) % drawn.shape[widest]] + spot[widest + 1:]
    return drawn.at[tuple(spot)].set(low).at[tuple(neighbour)].set(high)


def rank_table(count, slope):
    loads = [(1 << 20) // math.isqrt(rank ** slope) + 1 for rank in range(1, count + 1)]
    deviation = 1 + sum(loads) // (1 << 30)
    return np.cumsum(np.array([max(1, weight // deviation) for weight in loads]))


def skewed_ids(key, shape, count, lean):
    grid = rank_table(count, lean)
    pick = jax.random.randint(jax.random.fold_in(key, 1), shape, 0, int(grid[count - 1]))
    grade = jnp.searchsorted(jnp.asarray(grid, jnp.int32), pick, side="right")
    return jax.random.permutation(jax.random.fold_in(key, 2), count)[grade].astype(jnp.int32)


def setup_inputs(seed: int = 0) -> dict:
    seeds = jax.random.split(jax.random.key(seed), 5)
    return {
        "spectra": draw_spectra(jax.random.fold_in(seeds[4], 71), 0),
        "half_width": draw_half_width(jax.random.fold_in(seeds[4], 71), 0),
        "panel_block": touch_ends(skewed_ids(seeds[2], (NPANEL,), N_CHAN, 2), jax.random.fold_in(seeds[2], 3), 0, N_CHAN - 1).astype(jnp.int32),
        "panel_offset": touch_ends(jax.random.randint(seeds[3], (NPANEL,), 0, CH_DEV - PANEL + 1), jax.random.fold_in(seeds[3], 1), 0, CH_DEV - PANEL).astype(jnp.int32),
    }


def norm_scale(power, widths):
    padded = jnp.pad(power, ((HALO, HALO), (0, 0)))
    total = jnp.zeros_like(power)
    for offset in range(-HALO, HALO + 1):
        window = padded[HALO + offset:HALO + offset + CHANNELS]
        total = total + jnp.where(abs(offset) <= widths[None, :], window, jnp.float32(0.0))
    chan_index = jnp.arange(CHANNELS, dtype=jnp.int32)[:, None]
    count = jnp.minimum(chan_index + widths[None, :], CHANNELS - 1) - jnp.maximum(chan_index - widths[None, :], 0) + 1
    return lax.rsqrt(total / (count.astype(jnp.float32) * NF) + 1e-06)

def cross_bin(pair):
    normed_bin, source_bin = pair
    left = normed_bin.reshape(2 * CHANNELS, W).astype(jnp.float32)
    right = source_bin.reshape(2 * PANEL, W).astype(jnp.float32)
    grams = jnp.dot(left, right.T)
    real_part = grams[:CHANNELS, :PANEL] + grams[CHANNELS:, PANEL:]
    imag_part = grams[CHANNELS:, :PANEL] - grams[:CHANNELS, PANEL:]
    return (jnp.stack([real_part, imag_part]) * W ** (-0.5)).astype(jnp.bfloat16)

def reference(spectra, half_width, panel_block, panel_offset):
    values = spectra.astype(jnp.float32)
    power = lax.optimization_barrier(jnp.sum(values * values, axis=(0, 1)))
    scale = norm_scale(power, half_width)
    normed = (values * scale[None, None]).astype(jnp.bfloat16)
    results = []
    for panel in range(NPANEL):
        start = (panel_block[panel] * CH_DEV + panel_offset[panel]).astype(jnp.int32)
        source = lax.dynamic_slice_in_dim(normed, start, PANEL, 2)
        results.append(lax.map(cross_bin, (normed, source)))
    return jnp.stack(results)
```

```python
import functools

import jax
import jax.numpy as jnp
from jax import lax
from jax.experimental import pallas as pl
from jax.experimental.pallas import tpu as pltpu
from jax.sharding import PartitionSpec as P

PANEL = 256
NPANEL = 4
HALO = 32
HALF = PANEL // 2
LANES = 128
LAG = 2
PPC = 1


def edges_kernel(p_ref, q_ref, l0_ref, l1_ref, h0_ref, h1_ref, *outs):
    rows = p_ref.shape[0]
    for g, out in enumerate(outs):
        lanes = slice(g * LANES, (g + 1) * LANES)
        out[:HALO, :] = l0_ref[:, lanes] + l1_ref[:, lanes]
        out[HALO : HALO + rows, :] = p_ref[:, lanes] + q_ref[:, lanes]
        out[HALO + rows :, :] = h0_ref[:, lanes] + h1_ref[:, lanes]


def norm_kernel(slots, channels, bins, starts_ref, p_ref, q_ref, w_ref, x_ref, normed_ref, cut_ref, s_ref, t_ref, n_ref):
    f_dev, parts, rows, _ = x_ref.shape
    ext = rows + 2 * HALO
    width = w_ref[...]
    span = 2 * width + 1
    s_ref[:ext, :] = p_ref[...] + q_ref[...]
    s_ref[ext:, :] = jnp.zeros((s_ref.shape[0] - ext, LANES), jnp.float32)
    t_ref[...] = s_ref[...]
    step = 1
    while step * 2 <= 2 * HALO + 1:
        n = ext
        doubled = s_ref[0:n, :] + s_ref[step : step + n, :]
        s_ref[0:n, :] = doubled
        step *= 2
        here = t_ref[0:n, :]
        t_ref[0:n, :] = jnp.where((span & step) != 0, s_ref[0:n, :] + t_ref[step : step + n, :], here)
    skip = HALO - width
    step = 1
    n = ext
    while step < HALO:
        n = n - step
        t_ref[0:n, :] = jnp.where((skip & step) != 0, t_ref[step : step + n, :], t_ref[0:n, :])
        step *= 2
    total = t_ref[:rows, :]
    chan = lax.broadcasted_iota(jnp.int32, (rows, LANES), 0) + lax.axis_index("chan") * rows
    count = jnp.minimum(chan + width, channels - 1) - jnp.maximum(chan - width, 0) + 1
    scale = lax.rsqrt(total / (count.astype(jnp.float32) * bins) + 1e-06)
    for f in range(f_dev):
        for k in range(parts):
            value = (x_ref[f, k].astype(jnp.float32) * scale).astype(jnp.bfloat16)
            normed_ref[f, k] = value
            n_ref[f, k] = value.astype(jnp.float32)
    for j in range(slots):
        start = starts_ref[j]
        for f in range(f_dev):
            for k in range(parts):
                cut_ref[j, f, k] = n_ref[f, k, pl.ds(start, HALF), :].astype(jnp.bfloat16)


def cross_kernel(groups, scaling, *refs):
    normed = refs[:groups]
    mine = refs[groups : 2 * groups]
    other = refs[2 * groups : 3 * groups]
    out_ref, src_ref = refs[-2:]
    side = lax.rem(lax.axis_index("chan"), 2)
    here = pl.ds(pl.multiple_of(side * HALF, HALF), HALF)
    there = pl.ds(pl.multiple_of((1 - side) * HALF, HALF), HALF)
    for g in range(groups):
        lanes = slice(g * LANES, (g + 1) * LANES)
        for k in range(2):
            src_ref[k, here, lanes] = mine[g][0, 0, k]
            src_ref[k, there, lanes] = other[g][0, 0, k]
    left = [jnp.concatenate([n[0, k] for n in normed], axis=1) for k in range(2)]
    right = [src_ref[k] for k in range(2)]

    def dot(a, b):
        return lax.dot_general(a, b, (((1,), (1,)), ((), ())), preferred_element_type=jnp.float32)

    out_ref[0, 0, 0] = ((dot(left[0], right[0]) + dot(left[1], right[1])) * scaling).astype(jnp.bfloat16)
    out_ref[0, 0, 1] = ((dot(left[1], right[0]) - dot(left[0], right[1])) * scaling).astype(jnp.bfloat16)


def local(depth, spectra, half_width, panel_block, panel_offset):
    f_dev, parts, ch_dev, windows = spectra.shape
    n_chan, n_band = lax.axis_size("chan"), lax.axis_size("band")
    bins, channels = f_dev * n_band, ch_dev * n_chan
    groups = windows // LANES
    rows_z = n_chan // 2
    me = lax.axis_index("chan")
    z, x = me // 2, me % 2
    vmem = pl.BlockSpec(memory_space=pltpu.VMEM)

    blocks = jnp.broadcast_to(panel_block[:, None], (NPANEL, LANES))
    root_z = blocks // 2
    same = blocks[:, None, :] == blocks[None, :, :]
    earlier = jnp.arange(NPANEL)[:, None] > jnp.arange(NPANEL)[None, :]
    rank = jnp.sum((same & earlier[:, :, None]).astype(jnp.int32), axis=1)
    is_me = blocks == me
    rank1 = rank[:, 0]
    slot_start = [
        jnp.sum(jnp.where((panel_block == me) & (rank1 == j), panel_offset, 0)) + (1 - x) * HALF for j in range(depth)
    ]
    starts = jnp.concatenate([panel_offset + x * HALF, jnp.stack(slot_start)])

    power = jnp.sum(jnp.square(spectra.astype(jnp.float32)), axis=(0, 1))
    both = ("chan", "band")

    def shift(block, by, flip):
        pairs = [
            (c * n_band + b, (c + by) * n_band + (b ^ flip))
            for c in range(n_chan)
            for b in range(n_band)
            if 0 <= c + by < n_chan
        ]
        return lax.ppermute(block, both, pairs)

    def flip(block, bit):
        return lax.ppermute(block, "band", [(b, b ^ bit) for b in range(n_band)])

    low_edge, high_edge = power[:HALO], power[ch_dev - HALO :]
    q = flip(power, 1)
    halos = [shift(high_edge, 1, 0), shift(high_edge, 1, 1), shift(low_edge, -1, 0), shift(low_edge, -1, 1)]
    ext = ch_dev + 2 * HALO
    shares = pl.pallas_call(
        edges_kernel,
        out_shape=[jax.ShapeDtypeStruct((ext, LANES), jnp.float32)] * groups,
        in_specs=[vmem] * 6,
        out_specs=[vmem] * groups,
        name="edges",
    )(power, q, *halos)

    widths = half_width.reshape(1, windows)
    slots = NPANEL + depth
    normed, cuts = [], []
    for g in range(groups):
        p = shares[g]
        bit = 2
        while bit * 2 < n_band:
            p = p + flip(p, bit)
            bit *= 2
        n, cut = pl.pallas_call(
            functools.partial(norm_kernel, slots, channels, bins),
            grid=(1,),
            out_shape=[
                jax.ShapeDtypeStruct((f_dev, parts, ch_dev, LANES), jnp.bfloat16),
                jax.ShapeDtypeStruct((slots, f_dev, parts, HALF, LANES), jnp.bfloat16),
            ],
            in_specs=[
                pl.BlockSpec(memory_space=pltpu.SMEM),
                pl.BlockSpec((ext, LANES), lambda i: (0, 0)),
                pl.BlockSpec((ext, LANES), lambda i: (0, 0)),
                pl.BlockSpec((1, LANES), lambda i, g=g: (0, g)),
                pl.BlockSpec((f_dev, parts, ch_dev, LANES), lambda i, g=g: (0, 0, 0, g)),
            ],
            out_specs=[
                pl.BlockSpec((f_dev, parts, ch_dev, LANES), lambda i: (0, 0, 0, 0)),
                pl.BlockSpec((slots, f_dev, parts, HALF, LANES), lambda i: (0, 0, 0, 0, 0)),
            ],
            scratch_shapes=[
                pltpu.VMEM((ext + 2 * HALO, LANES), jnp.float32),
                pltpu.VMEM((ext + 2 * HALO, LANES), jnp.float32),
                pltpu.VMEM((f_dev, parts, ch_dev, LANES), jnp.float32),
            ],
            name=f"norm{g}",
        )(starts, p, flip(p, bit), widths, spectra)
        normed.append(n)
        cuts.append(cut)

    def lanes_of(mask):
        return mask[:, None, None, None, :]

    rung = [(c, c ^ 1) for c in range(n_chan)]
    per = NPANEL // PPC
    n_chunks = groups * per
    panels = [slice((c % per) * PPC, (c % per + 1) * PPC) for c in range(n_chunks)]
    init = []
    for g in range(groups):
        got = [lax.ppermute(cuts[g][NPANEL + j][None], "chan", rung) for j in range(depth)]
        for i in range(per):
            ps = slice(i * PPC, (i + 1) * PPC)
            value = got[0]
            for j in range(1, depth):
                value = jnp.where(lanes_of(rank[ps] == j), got[j], value)
            init.append(jnp.where(lanes_of(is_me[ps]), cuts[g][ps], value))

    def chain(order):
        before = (lambda p, r: root_z[p] < r) if order[0] == 0 else (lambda p, r: root_z[p] > r)
        got = []
        for t in range(n_chunks + LAG * (rows_z - 2)):
            value, pairs = None, []
            for hop in range(rows_z - 1):
                c = t - LAG * hop
                if not 0 <= c < n_chunks:
                    continue
                r, to = order[hop], order[hop + 1]
                pairs += [(2 * r + s, 2 * to + s) for s in range(2)]
                item = init[c]
                if hop:
                    item = jnp.where(lanes_of(before(panels[c], r)), got[t - LAG], item)
                value = item if value is None else jnp.where(z == r, item, value)
            got.append(lax.ppermute(value, "chan", pairs))
        return got

    ups, downs = chain(list(range(rows_z))), chain(list(range(rows_z))[::-1])
    mine, other = [], []
    for c in range(n_chunks):
        value = init[c]
        for r in range(1, rows_z):
            value = jnp.where((z == r) & lanes_of(root_z[panels[c]] < r), ups[c + LAG * (r - 1)], value)
        for r in range(rows_z - 1):
            value = jnp.where((z == r) & lanes_of(root_z[panels[c]] > r), downs[c + LAG * (rows_z - 2 - r)], value)
        mine.append(value)
        other.append(lax.ppermute(value, "chan", rung))

    out = None
    for p in range(NPANEL):
        at = [(g * per + p // PPC, p % PPC) for g in range(groups)]
        piece = pl.BlockSpec((1, 1, parts, HALF, LANES), lambda f, i=p % PPC: (i, f, 0, 0, 0))
        args = normed + [mine[c] for c, _ in at] + [other[c] for c, _ in at]
        specs = [pl.BlockSpec((1, parts, ch_dev, LANES), lambda f: (f, 0, 0, 0))] * groups + [piece] * (2 * groups)
        aliases = {}
        if out is not None:
            aliases = {len(args): 0}
            args.append(out)
            specs.append(pl.BlockSpec(memory_space=pl.ANY))
        out = pl.pallas_call(
            functools.partial(cross_kernel, groups, windows ** (-0.5)),
            grid=(f_dev,),
            out_shape=jax.ShapeDtypeStruct((NPANEL, f_dev, parts, ch_dev, PANEL), jnp.bfloat16),
            in_specs=specs,
            out_specs=pl.BlockSpec((1, 1, parts, ch_dev, PANEL), lambda f, p=p: (p, f, 0, 0, 0)),
            scratch_shapes=[pltpu.VMEM((parts, PANEL, windows), jnp.bfloat16)],
            input_output_aliases=aliases,
            name=f"cross{p}",
        )(*args)
    return out


def solution(mesh):
    placed = (P("band", None, "chan", None), P(), P(), P())
    return jax.shard_map(
        functools.partial(local, NPANEL),
        mesh=mesh,
        in_specs=placed,
        out_specs=P(None, "band", None, "chan", None),
        check_vma=False,
    )
```

```python
import functools

import jax
import jax.numpy as jnp
from jax import lax
from jax.experimental import pallas as pl
from jax.experimental.pallas import tpu as pltpu
from jax.sharding import PartitionSpec as P

PANEL = 256
NPANEL = 4
HALO = 32
HALF = PANEL // 2
LANES = 128
LAG = 2
SUBS = 4


def edges_kernel(p_ref, q_ref, l0_ref, l1_ref, h0_ref, h1_ref, *outs):
    rows = p_ref.shape[0]
    for g, out in enumerate(outs):
        lanes = slice(g * LANES, (g + 1) * LANES)
        out[:HALO, :] = l0_ref[:, lanes] + l1_ref[:, lanes]
        out[HALO : HALO + rows, :] = p_ref[:, lanes] + q_ref[:, lanes]
        out[HALO + rows :, :] = h0_ref[:, lanes] + h1_ref[:, lanes]


def norm_kernel(subs, channels, bins, starts_ref, p_ref, q_ref, w_ref, x_ref, normed_ref, *rest):
    own, (s_ref, t_ref, n_ref) = rest[:-3], rest[-3:]
    f_dev, parts, rows, _ = x_ref.shape
    ext = rows + 2 * HALO
    width = w_ref[...]
    span = 2 * width + 1
    s_ref[:ext, :] = p_ref[...] + q_ref[...]
    s_ref[ext:, :] = jnp.zeros((s_ref.shape[0] - ext, LANES), jnp.float32)
    t_ref[...] = s_ref[...]
    step = 1
    while step * 2 <= 2 * HALO + 1:
        doubled = s_ref[0:ext, :] + s_ref[step : step + ext, :]
        s_ref[0:ext, :] = doubled
        step *= 2
        here = t_ref[0:ext, :]
        t_ref[0:ext, :] = jnp.where((span & step) != 0, doubled + t_ref[step : step + ext, :], here)
    skip = HALO - width
    step = 1
    n = ext
    while step < HALO:
        n = n - step
        t_ref[0:n, :] = jnp.where((skip & step) != 0, t_ref[step : step + n, :], t_ref[0:n, :])
        step *= 2
    total = t_ref[:rows, :]
    chan = lax.broadcasted_iota(jnp.int32, (rows, LANES), 0) + lax.axis_index("chan") * rows
    count = jnp.minimum(chan + width, channels - 1) - jnp.maximum(chan - width, 0) + 1
    scale = lax.rsqrt(total / (count.astype(jnp.float32) * bins) + 1e-06)
    for f in range(f_dev):
        for k in range(parts):
            value = (x_ref[f, k].astype(jnp.float32) * scale).astype(jnp.bfloat16)
            normed_ref[f, k] = value
            n_ref[f, k] = value.astype(jnp.float32)
    size = HALF // subs
    for p in range(NPANEL):
        start = starts_ref[p]
        for half in range(2):
            for j in range(subs):
                at = pl.ds(start + (half * HALF + j * size), size)
                for f in range(f_dev):
                    for k in range(parts):
                        own[half * subs + j][p, f, k] = n_ref[f, k, at, :].astype(jnp.bfloat16)


def cross_kernel(groups, n_chan, n_chunks, n_steps, scaling, table_ref, *refs):
    normed, refs = refs[:groups], refs[groups:]
    lists = []
    for size in (n_chunks, n_chunks, n_steps, n_steps):
        lists.append(refs[:size])
        refs = refs[size:]
    out_ref, src_ref, sems = refs
    per = n_chunks // groups
    size = HALF // per
    p = pl.program_id(0)

    def each(panel, slot, do):
        for half in range(2):
            away = table_ref[half * NPANEL + panel]
            for d in range(n_chan):

                @pl.when(away == d)
                def _():
                    for c in range(n_chunks):
                        g, j = c // per, c % per
                        source = lists[half][c] if d == 0 else lists[2 + half][c + LAG * (d - 1)]
                        do(
                            pltpu.make_async_copy(
                                source.at[panel],
                                src_ref.at[slot, :, :, pl.ds(half * HALF + j * size, size), pl.ds(g * LANES, LANES)],
                                sems.at[slot],
                            )
                        )

    slot = lax.rem(p, 2)

    @pl.when(p == 0)
    def _():
        each(0, 0, lambda copy: copy.start())

    pltpu.make_async_copy(src_ref.at[slot], src_ref.at[slot], sems.at[slot]).wait()

    @pl.when(p + 1 < NPANEL)
    def _():
        each(p + 1, 1 - slot, lambda copy: copy.start())

    def dot(a, b):
        return lax.dot_general(a, b, (((1,), (1,)), ((), ())), preferred_element_type=jnp.float32)

    for f in range(src_ref.shape[1]):
        left = [jnp.concatenate([n[f, k] for n in normed], axis=1) for k in range(2)]
        right = [src_ref[slot, f, k] for k in range(2)]
        out_ref[0, f, 0] = ((dot(left[0], right[0]) + dot(left[1], right[1])) * scaling).astype(jnp.bfloat16)
        out_ref[0, f, 1] = ((dot(left[1], right[0]) - dot(left[0], right[1])) * scaling).astype(jnp.bfloat16)


def local(spectra, half_width, panel_block, panel_offset):
    f_dev, parts, ch_dev, windows = spectra.shape
    n_chan, n_band = lax.axis_size("chan"), lax.axis_size("band")
    bins, channels = f_dev * n_band, ch_dev * n_chan
    groups = windows // LANES
    me = lax.axis_index("chan")
    vmem = pl.BlockSpec(memory_space=pltpu.VMEM)
    hbm = pl.BlockSpec(memory_space=pl.ANY)

    ring = list(range(0, n_chan, 2)) + list(range(1, n_chan, 2))[::-1]

    def place(c):
        return jnp.where(c % 2 == 0, c // 2, n_chan - 1 - c // 2)

    ahead = lax.rem(place(me) - place(panel_block) + n_chan, n_chan)
    table = jnp.concatenate([ahead, lax.rem(n_chan - ahead, n_chan)])
    is_me = jnp.broadcast_to((panel_block == me)[:, None, None, None, None], (NPANEL, 1, 1, 1, LANES))

    power = jnp.sum(jnp.square(spectra.astype(jnp.float32)), axis=(0, 1))
    both = ("chan", "band")

    def shift(block, by, flip):
        pairs = [
            (c * n_band + b, (c + by) * n_band + (b ^ flip))
            for c in range(n_chan)
            for b in range(n_band)
            if 0 <= c + by < n_chan
        ]
        return lax.ppermute(block, both, pairs)

    def flip(block, bit):
        return lax.ppermute(block, "band", [(b, b ^ bit) for b in range(n_band)])

    low_edge, high_edge = power[:HALO], power[ch_dev - HALO :]
    q = flip(power, 1)
    halos = [shift(high_edge, 1, 0), shift(high_edge, 1, 1), shift(low_edge, -1, 0), shift(low_edge, -1, 1)]
    ext = ch_dev + 2 * HALO
    shares = pl.pallas_call(
        edges_kernel,
        out_shape=[jax.ShapeDtypeStruct((ext, LANES), jnp.float32)] * groups,
        in_specs=[vmem] * 6,
        out_specs=[vmem] * groups,
        name="edges",
    )(power, q, *halos)

    widths = half_width.reshape(1, windows)
    piece = (NPANEL, f_dev, parts, HALF // SUBS, LANES)
    normed, own = [], [[], []]
    for g in range(groups):
        p = shares[g]
        bit = 2
        while bit * 2 < n_band:
            p = p + flip(p, bit)
            bit *= 2
        n, *cut = pl.pallas_call(
            functools.partial(norm_kernel, SUBS, channels, bins),
            grid=(1,),
            out_shape=[jax.ShapeDtypeStruct((f_dev, parts, ch_dev, LANES), jnp.bfloat16)]
            + [jax.ShapeDtypeStruct(piece, jnp.bfloat16)] * (2 * SUBS),
            in_specs=[
                pl.BlockSpec(memory_space=pltpu.SMEM),
                pl.BlockSpec((ext, LANES), lambda i: (0, 0)),
                pl.BlockSpec((ext, LANES), lambda i: (0, 0)),
                pl.BlockSpec((1, LANES), lambda i, g=g: (0, g)),
                pl.BlockSpec((f_dev, parts, ch_dev, LANES), lambda i, g=g: (0, 0, 0, g)),
            ],
            out_specs=[vmem] * (1 + 2 * SUBS),
            scratch_shapes=[
                pltpu.VMEM((ext + 2 * HALO, LANES), jnp.float32),
                pltpu.VMEM((ext + 2 * HALO, LANES), jnp.float32),
                pltpu.VMEM((f_dev, parts, ch_dev, LANES), jnp.float32),
            ],
            name=f"norm{g}",
        )(panel_offset, p, flip(p, bit), widths, spectra)
        normed.append(n)
        own[0] += cut[:SUBS]
        own[1] += cut[SUBS:]

    n_chunks = groups * SUBS
    n_steps = n_chunks + LAG * (n_chan - 2)
    got = [[], []]
    for t in range(n_steps):
        for half in range(2):
            value = own[half][t] if t < n_chunks else got[half][t - LAG]
            if LAG <= t < n_chunks:
                value = jnp.where(is_me, value, got[half][t - LAG])
            step = 1 if half == 0 else -1
            pairs = [(ring[i], ring[(i + step) % n_chan]) for i in range(n_chan)]
            got[half].append(lax.ppermute(value, "chan", pairs))

    block = (1, f_dev, parts, ch_dev, PANEL)
    return pl.pallas_call(
        functools.partial(cross_kernel, groups, n_chan, n_chunks, n_steps, windows ** (-0.5)),
        grid=(NPANEL,),
        out_shape=jax.ShapeDtypeStruct((NPANEL, f_dev, parts, ch_dev, PANEL), jnp.bfloat16),
        in_specs=[pl.BlockSpec(memory_space=pltpu.SMEM)]
        + [pl.BlockSpec((f_dev, parts, ch_dev, LANES), lambda p: (0, 0, 0, 0))] * groups
        + [hbm] * (2 * n_chunks + 2 * n_steps),
        out_specs=pl.BlockSpec(block, lambda p: (p, 0, 0, 0, 0)),
        scratch_shapes=[
            pltpu.VMEM((2, f_dev, parts, PANEL, windows), jnp.bfloat16),
            pltpu.SemaphoreType.DMA((2,)),
        ],
        name="cross",
    )(table, *normed, *own[0], *own[1], *got[0], *got[1])


def solution(mesh):
    placed = (P("band", None, "chan", None), P(), P(), P())
    return jax.shard_map(
        local,
        mesh=mesh,
        in_specs=placed,
        out_specs=P(None, "band", None, "chan", None),
        check_vma=False,
    )
```

```python
import functools

import jax
import jax.numpy as jnp
from jax import lax
from jax.experimental import pallas as pl
from jax.experimental.pallas import tpu as pltpu
from jax.sharding import PartitionSpec as P


PANEL = 256
NPANEL = 4
HALO = 32
HALF = PANEL // 2
LANES = 128
LAG = 2
SUBS = 4


def edges_kernel(p_ref, q_ref, l0_ref, l1_ref, h0_ref, h1_ref, *outs):
    rows = p_ref.shape[0]
    for g, out in enumerate(outs):
        lanes = slice(g * LANES, (g + 1) * LANES)
        out[:HALO, :] = l0_ref[:, lanes] + l1_ref[:, lanes]
        out[HALO : HALO + rows, :] = p_ref[:, lanes] + q_ref[:, lanes]
        out[HALO + rows :, :] = h0_ref[:, lanes] + h1_ref[:, lanes]


def norm_kernel(subs, channels, bins, starts_ref, p_ref, q_ref, w_ref, x_ref, normed_ref, *rest):
    own, (s_ref, t_ref, n_ref) = rest[:-3], rest[-3:]
    f_dev, parts, rows, _ = x_ref.shape
    ext = rows + 2 * HALO
    width = w_ref[...]
    span = 2 * width + 1
    s_ref[:ext, :] = p_ref[...] + q_ref[...]
    s_ref[ext:, :] = jnp.zeros((s_ref.shape[0] - ext, LANES), jnp.float32)
    t_ref[...] = s_ref[...]
    step = 1
    while step * 2 <= 2 * HALO + 1:
        doubled = s_ref[0:ext, :] + s_ref[step : step + ext, :]
        s_ref[0:ext, :] = doubled
        step *= 2
        here = t_ref[0:ext, :]
        t_ref[0:ext, :] = jnp.where((span & step) != 0, doubled + t_ref[step : step + ext, :], here)
    skip = HALO - width
    step = 1
    n = ext
    while step < HALO:
        n = n - step
        t_ref[0:n, :] = jnp.where((skip & step) != 0, t_ref[step : step + n, :], t_ref[0:n, :])
        step *= 2
    total = t_ref[:rows, :]
    chan = lax.broadcasted_iota(jnp.int32, (rows, LANES), 0) + lax.axis_index("chan") * rows
    count = jnp.minimum(chan + width, channels - 1) - jnp.maximum(chan - width, 0) + 1
    scale = lax.rsqrt(total / (count.astype(jnp.float32) * bins) + 1e-06)
    for f in range(f_dev):
        for k in range(parts):
            value = (x_ref[f, k].astype(jnp.float32) * scale).astype(jnp.bfloat16)
            normed_ref[f, k] = value
            n_ref[f, k] = value.astype(jnp.float32)
    size = HALF // subs
    for p in range(NPANEL):
        start = starts_ref[p]
        for half in range(2):
            for j in range(subs):
                at = pl.ds(start + (half * HALF + j * size), size)
                for f in range(f_dev):
                    for k in range(parts):
                        own[half * subs + j][p, f, k] = n_ref[f, k, at, :].astype(jnp.bfloat16)


def pick_kernel(mine_ref, a_ref, b_ref, c_ref, d_ref, out0, out1):
    size = a_ref.shape[-2]
    for p in range(NPANEL):
        mask = jnp.broadcast_to(mine_ref[p, 0:1, :], (size, LANES)) > 0
        for f in range(a_ref.shape[1]):
            for k in range(a_ref.shape[2]):
                out0[p, f, k] = jnp.where(mask, a_ref[p, f, k], c_ref[p, f, k])
                out1[p, f, k] = jnp.where(mask, b_ref[p, f, k], d_ref[p, f, k])


def cross_kernel(groups, n_chan, n_chunks, n_steps, scaling, table_ref, *refs):
    normed, refs = refs[:groups], refs[groups:]
    lists = []
    for size in (n_chunks, n_chunks, n_steps, n_steps):
        lists.append(refs[:size])
        refs = refs[size:]
    out_ref, src_ref, sems = refs
    per = n_chunks // groups
    size = HALF // per
    p = pl.program_id(0)

    def each(panel, slot, do):
        for half in range(2):
            away = table_ref[half * NPANEL + panel]
            for d in range(n_chan):

                @pl.when(away == d)
                def _():
                    for c in range(n_chunks):
                        g, j = c // per, c % per
                        source = lists[half][c] if d == 0 else lists[2 + half][c + LAG * (d - 1)]
                        do(
                            pltpu.make_async_copy(
                                source.at[panel],
                                src_ref.at[slot, :, :, pl.ds(half * HALF + j * size, size), pl.ds(g * LANES, LANES)],
                                sems.at[slot],
                            )
                        )

    slot = lax.rem(p, 2)

    @pl.when(p == 0)
    def _():
        each(0, 0, lambda copy: copy.start())

    pltpu.make_async_copy(src_ref.at[slot], src_ref.at[slot], sems.at[slot]).wait()

    @pl.when(p + 1 < NPANEL)
    def _():
        each(p + 1, 1 - slot, lambda copy: copy.start())

    def dot(a, b):
        return lax.dot_general(a, b, (((1,), (1,)), ((), ())), preferred_element_type=jnp.float32)

    for f in range(src_ref.shape[1]):
        left = [jnp.concatenate([n[f, k] for n in normed], axis=1) for k in range(2)]
        right = [src_ref[slot, f, k] for k in range(2)]
        out_ref[0, f, 0] = ((dot(left[0], right[0]) + dot(left[1], right[1])) * scaling).astype(jnp.bfloat16)
        out_ref[0, f, 1] = ((dot(left[1], right[0]) - dot(left[0], right[1])) * scaling).astype(jnp.bfloat16)


def local(spectra, half_width, panel_block, panel_offset):
    f_dev, parts, ch_dev, windows = spectra.shape
    n_chan, n_band = lax.axis_size("chan"), lax.axis_size("band")
    bins, channels = f_dev * n_band, ch_dev * n_chan
    groups = windows // LANES
    me = lax.axis_index("chan")
    vmem = pl.BlockSpec(memory_space=pltpu.VMEM)
    hbm = pl.BlockSpec(memory_space=pl.ANY)

    ring = list(range(0, n_chan, 2)) + list(range(1, n_chan, 2))[::-1]

    def place(c):
        return jnp.where(c % 2 == 0, c // 2, n_chan - 1 - c // 2)

    ahead = lax.rem(place(me) - place(panel_block) + n_chan, n_chan)
    table = jnp.concatenate([ahead, lax.rem(n_chan - ahead, n_chan)])
    mine = jnp.broadcast_to((panel_block == me)[:, None, None].astype(jnp.float32), (NPANEL, 8, LANES))

    power = jnp.sum(jnp.square(spectra.astype(jnp.float32)), axis=(0, 1))
    both = ("chan", "band")

    def shift(block, by, flip):
        pairs = [
            (c * n_band + b, (c + by) * n_band + (b ^ flip))
            for c in range(n_chan)
            for b in range(n_band)
            if 0 <= c + by < n_chan
        ]
        return lax.ppermute(block, both, pairs)

    def flip(block, bit):
        return lax.ppermute(block, "band", [(b, b ^ bit) for b in range(n_band)])

    low_edge, high_edge = power[:HALO], power[ch_dev - HALO :]
    q = flip(power, 1)
    halos = [shift(high_edge, 1, 0), shift(high_edge, 1, 1), shift(low_edge, -1, 0), shift(low_edge, -1, 1)]
    ext = ch_dev + 2 * HALO
    shares = pl.pallas_call(
        edges_kernel,
        out_shape=[jax.ShapeDtypeStruct((ext, LANES), jnp.float32)] * groups,
        in_specs=[vmem] * 6,
        out_specs=[vmem] * groups,
        name="edges",
    )(power, q, *halos)

    widths = half_width.reshape(1, windows)
    piece = (NPANEL, f_dev, parts, HALF // SUBS, LANES)
    normed, own = [], [[], []]
    for g in range(groups):
        p = shares[g]
        bit = 2
        while bit * 2 < n_band:
            p = p + flip(p, bit)
            bit *= 2
        n, *cut = pl.pallas_call(
            functools.partial(norm_kernel, SUBS, channels, bins),
            grid=(1,),
            out_shape=[jax.ShapeDtypeStruct((f_dev, parts, ch_dev, LANES), jnp.bfloat16)]
            + [jax.ShapeDtypeStruct(piece, jnp.bfloat16)] * (2 * SUBS),
            in_specs=[
                pl.BlockSpec(memory_space=pltpu.SMEM),
                pl.BlockSpec((ext, LANES), lambda i: (0, 0)),
                pl.BlockSpec((ext, LANES), lambda i: (0, 0)),
                pl.BlockSpec((1, LANES), lambda i, g=g: (0, g)),
                pl.BlockSpec((f_dev, parts, ch_dev, LANES), lambda i, g=g: (0, 0, 0, g)),
            ],
            out_specs=[vmem] * (1 + 2 * SUBS),
            scratch_shapes=[
                pltpu.VMEM((ext + 2 * HALO, LANES), jnp.float32),
                pltpu.VMEM((ext + 2 * HALO, LANES), jnp.float32),
                pltpu.VMEM((f_dev, parts, ch_dev, LANES), jnp.float32),
            ],
        )(panel_offset, p, flip(p, bit), widths, spectra)
        normed.append(n)
        own[0] += cut[:SUBS]
        own[1] += cut[SUBS:]

    n_chunks = groups * SUBS
    n_steps = n_chunks + LAG * (n_chan - 2)
    got = [[], []]
    for t in range(n_steps):
        if t < LAG:
            value = [own[half][t] for half in range(2)]
        elif t < n_chunks:
            value = pl.pallas_call(
                pick_kernel,
                out_shape=[jax.ShapeDtypeStruct(piece, jnp.bfloat16)] * 2,
                in_specs=[vmem] * 5,
                out_specs=[vmem] * 2,
                name="pick",
            )(mine, own[0][t], own[1][t], got[0][t - LAG], got[1][t - LAG])
        else:
            value = [got[half][t - LAG] for half in range(2)]
        for half in range(2):
            step = 1 if half == 0 else -1
            pairs = [(ring[i], ring[(i + step) % n_chan]) for i in range(n_chan)]
            got[half].append(lax.ppermute(value[half], "chan", pairs))

    block = (1, f_dev, parts, ch_dev, PANEL)
    return pl.pallas_call(
        functools.partial(cross_kernel, groups, n_chan, n_chunks, n_steps, windows ** (-0.5)),
        grid=(NPANEL,),
        out_shape=jax.ShapeDtypeStruct((NPANEL, f_dev, parts, ch_dev, PANEL), jnp.bfloat16),
        in_specs=[pl.BlockSpec(memory_space=pltpu.SMEM)]
        + [pl.BlockSpec((f_dev, parts, ch_dev, LANES), lambda p: (0, 0, 0, 0))] * groups
        + [hbm] * (2 * n_chunks + 2 * n_steps),
        out_specs=pl.BlockSpec(block, lambda p: (p, 0, 0, 0, 0)),
        scratch_shapes=[
            pltpu.VMEM((2, f_dev, parts, PANEL, windows), jnp.bfloat16),
            pltpu.SemaphoreType.DMA((2,)),
        ],
        name="cross",
    )(table, *normed, *own[0], *own[1], *got[0], *got[1])


def solution(mesh):
    placed = (P("band", None, "chan", None), P(), P(), P())
    return jax.shard_map(
        local,
        mesh=mesh,
        in_specs=placed,
        out_specs=P(None, "band", None, "chan", None),
        check_vma=False,
    )
```

```python
import functools

import jax
import jax.numpy as jnp
from jax import lax
from jax.experimental import pallas as pl
from jax.experimental.pallas import tpu as pltpu
from jax.sharding import PartitionSpec as P


PANEL = 256
NPANEL = 4
HALO = 32
HALF = PANEL // 2
LANES = 128
LAG = 2
SUBS = 4
SPANS = (1, 3)


def spans_of(groups):
    counts = SPANS if sum(SPANS) == groups else (groups,)
    return [(sum(counts[:i]), n) for i, n in enumerate(counts)]


def plan(n_chan, n_chunks):
    both = min(LAG * (n_chan // 2 - 1) // 2, n_chunks)
    single = n_chunks - both
    n_sends = single + 2 * both
    return single, n_sends, max(single + LAG * (n_chan - 2), n_sends + LAG * (n_chan // 2 - 1))


def scale_kernel(channels, bins, p_ref, q_ref, h0_ref, h1_ref, w_ref, scale_ref, s_ref, t_ref):
    rows, _ = scale_ref.shape
    ext = rows + 2 * HALO
    far = lax.rem(lax.axis_index("band"), 2)
    width = w_ref[...]
    span = 2 * width + 1
    inner = p_ref[...] + q_ref[...]
    edge = h0_ref[...] + h1_ref[...]

    @pl.when(far == 0)
    def _():
        s_ref[:HALO, :] = edge
        s_ref[HALO:ext, :] = inner

    @pl.when(far == 1)
    def _():
        s_ref[: ext - HALO, :] = inner
        s_ref[ext - HALO : ext, :] = edge

    s_ref[ext:, :] = jnp.zeros((s_ref.shape[0] - ext, s_ref.shape[1]), jnp.float32)
    t_ref[...] = s_ref[...]
    step = 1
    while step * 2 <= 2 * HALO + 1:
        doubled = s_ref[0:ext, :] + s_ref[step : step + ext, :]
        s_ref[0:ext, :] = doubled
        step *= 2
        here = t_ref[0:ext, :]
        t_ref[0:ext, :] = jnp.where((span & step) != 0, doubled + t_ref[step : step + ext, :], here)
    skip = HALO - width
    step = 1
    n = ext
    while step < HALO:
        n = n - step
        t_ref[0:n, :] = jnp.where((skip & step) != 0, t_ref[step : step + n, :], t_ref[0:n, :])
        step *= 2
    total = t_ref[:rows, :]
    chan = lax.broadcasted_iota(jnp.int32, scale_ref.shape, 0) + (2 * lax.axis_index("chan") + far) * rows
    count = jnp.minimum(chan + width, channels - 1) - jnp.maximum(chan - width, 0) + 1
    scale_ref[...] = lax.rsqrt(total / (count.astype(jnp.float32) * bins) + 1e-06)


def norm_kernel(base, groups, subs, starts_ref, mine_ref, other_ref, x_ref, *rest):
    per = 2 * subs
    normed, own = rest[:groups], rest[groups : groups * (1 + per)]
    x_buf, scale_buf, normed_buf, n_ref, in_sem, scale_sem, out_sem = rest[groups * (1 + per) :]
    _, f_dev, parts, rows, _ = x_buf.shape
    half_rows = rows // 2
    far = lax.rem(lax.axis_index("band"), 2)
    reads = []
    for g in range(groups):
        lanes = pl.ds((base + g) * LANES, LANES)
        reads.append(pltpu.make_async_copy(x_ref.at[:, :, :, lanes], x_buf.at[g], in_sem.at[g]))
        reads[g].start()
    shares = []
    for i, ref in enumerate((mine_ref, other_ref)):
        at = far * half_rows if i == 0 else (1 - far) * half_rows
        at = pl.ds(pl.multiple_of(at, half_rows), half_rows)
        shares.append(pltpu.make_async_copy(ref, scale_buf.at[at, :], scale_sem.at[i]))
        shares[i].start()
    for copy in shares:
        copy.wait()
    size = HALF // subs
    writes = []
    for g in range(groups):
        reads[g].wait()
        scale = scale_buf[:, g * LANES : (g + 1) * LANES]
        for f in range(f_dev):
            for k in range(parts):
                value = (x_buf[g, f, k].astype(jnp.float32) * scale).astype(jnp.bfloat16)
                normed_buf[g, f, k] = value
                n_ref[f, k] = value.astype(jnp.float32)
        for p in range(NPANEL):
            start = starts_ref[p]
            for i in range(per):
                at = pl.ds(start + i * size, size)
                for f in range(f_dev):
                    for k in range(parts):
                        own[g * per + i][p, f, k] = n_ref[f, k, at, :].astype(jnp.bfloat16)
        writes.append(pltpu.make_async_copy(normed_buf.at[g], normed[g], out_sem.at[g]))
        writes[g].start()
    for copy in writes:
        copy.wait()


def cross_kernel(groups, n_chan, n_chunks, n_steps, single, scaling, block_ref, *refs):
    normed, refs = refs[:groups], refs[groups:]
    lists = []
    for size in (n_chunks, n_chunks, n_steps, n_steps):
        lists.append(refs[:size])
        refs = refs[size:]
    out_ref, src_ref, left_ref, sems, left_sem = refs
    per = n_chunks // groups
    size = HALF // per
    p = pl.program_id(0)

    def place(c):
        return jnp.where(lax.rem(c, 2) == 0, c // 2, n_chan - 1 - c // 2)

    here = place(lax.axis_index("chan"))

    def each(panel, slot, do):
        ahead = lax.rem(here - place(block_ref[panel]) + n_chan, n_chan)
        for d in range(n_chan):

            @pl.when(ahead == d)
            def _():
                for half in range(2):
                    for c in range(n_chunks):
                        g, j = c // per, c % per
                        if d == 0:
                            source = lists[half][c]
                        elif c < single:
                            source = lists[2 + half][c + LAG * ((d if half == 0 else n_chan - d) - 1)]
                        else:
                            t = single + 2 * (c - single) + half
                            way = 0 if d <= n_chan // 2 else 1
                            source = lists[2 + way][t + LAG * ((d if way == 0 else n_chan - d) - 1)]
                        do(
                            pltpu.make_async_copy(
                                source.at[panel],
                                src_ref.at[slot, :, :, g, pl.ds(half * HALF + j * size, size), :],
                                sems.at[slot],
                            )
                        )

    slot = lax.rem(p, 2)

    @pl.when(p == 0)
    def _():
        each(0, 0, lambda copy: copy.start())
        copies = [pltpu.make_async_copy(n, left_ref.at[g], left_sem.at[g]) for g, n in enumerate(normed)]
        for copy in copies:
            copy.start()
        for copy in copies:
            copy.wait()

    pltpu.make_async_copy(src_ref.at[slot], src_ref.at[slot], sems.at[slot]).wait()

    @pl.when(p + 1 < NPANEL)
    def _():
        each(p + 1, 1 - slot, lambda copy: copy.start())

    def dot(a, b):
        return lax.dot_general(a, b, (((1,), (1,)), ((), ())), preferred_element_type=jnp.float32)

    for f in range(src_ref.shape[1]):
        left = [[left_ref[g, f, k] for g in range(groups)] for k in range(2)]
        right = jnp.concatenate([src_ref[slot, f, k, g] for k in range(2) for g in range(groups)], axis=1)
        real = dot(jnp.concatenate(left[0] + left[1], axis=1), right)
        out_ref[0, f, 0] = (real * scaling).astype(jnp.bfloat16)
        imag = dot(jnp.concatenate(left[1] + [-n for n in left[0]], axis=1), right)
        out_ref[0, f, 1] = (imag * scaling).astype(jnp.bfloat16)


def local(spectra, half_width, panel_block, panel_offset):
    f_dev, parts, ch_dev, windows = spectra.shape
    n_chan, n_band = lax.axis_size("chan"), lax.axis_size("band")
    bins, channels = f_dev * n_band, ch_dev * n_chan
    groups = windows // LANES
    me = lax.axis_index("chan")
    hbm = pl.BlockSpec(memory_space=pl.ANY)

    ring = list(range(0, n_chan, 2)) + list(range(1, n_chan, 2))[::-1]

    is_me = jnp.broadcast_to((panel_block == me)[:, None, None, None, None], (NPANEL, 1, 1, 1, LANES))
    is_me = is_me.astype(jnp.float32)

    half_rows = ch_dev // 2
    keep_rows = half_rows + HALO
    band = lax.axis_index("band")
    near = band % 2 == 0

    def flip(block, bit):
        return lax.ppermute(block, "band", [(b, b ^ bit) for b in range(n_band)])

    def outward(block, bit):
        pairs = [
            (c * n_band + b, (c + (2 * (b % 2) - 1)) * n_band + (b ^ 1 ^ bit))
            for c in range(n_chan)
            for b in range(n_band)
            if 0 <= c + (2 * (b % 2) - 1) < n_chan
        ]
        return lax.ppermute(block, ("chan", "band"), pairs)

    power = jnp.sum(jnp.square(spectra.astype(jnp.float32)), axis=(0, 1))
    first, second = power[:keep_rows], power[half_rows - HALO :]
    share = jnp.where(near, first, second) + flip(jnp.where(near, second, first), 1)
    bit = 2
    while bit * 2 < n_band:
        share = share + flip(share, bit)
        bit *= 2
    spans = spans_of(groups)
    shares = [share[:, base * LANES : (base + n) * LANES] for base, n in spans]
    theirs = []
    for i in range(len(spans)):
        theirs.append(flip(shares[i], bit))
    edge = jnp.where(near, share[:HALO], share[keep_rows - HALO :])
    halos = [outward(edge, 0), outward(edge, bit)]
    widths = half_width.reshape(1, windows)

    piece = (NPANEL, f_dev, parts, HALF // SUBS, LANES)
    block = (f_dev, parts, ch_dev, LANES)
    cuts = 2 * SUBS
    normed, own = [], [[], []]
    for i, (base, n_groups) in enumerate(spans):
        span = n_groups * LANES
        scale = pl.pallas_call(
            functools.partial(scale_kernel, channels, bins),
            grid=(n_groups,),
            out_shape=jax.ShapeDtypeStruct((half_rows, span), jnp.float32),
            in_specs=[pl.BlockSpec((keep_rows, LANES), lambda g: (0, g))] * 2
            + [pl.BlockSpec((HALO, LANES), lambda g, base=base: (0, base + g))] * 2
            + [pl.BlockSpec((1, LANES), lambda g, base=base: (0, base + g))],
            out_specs=pl.BlockSpec((half_rows, LANES), lambda g: (0, g)),
            scratch_shapes=[pltpu.VMEM((half_rows + 4 * HALO, LANES), jnp.float32)] * 2,
            name="scale",
        )
        scale = scale(shares[i], theirs[i], *halos, widths)
        norm = pl.pallas_call(
            functools.partial(norm_kernel, base, n_groups, SUBS),
            out_shape=[jax.ShapeDtypeStruct(block, jnp.bfloat16)] * n_groups
            + [pltpu.VMEM(piece, jnp.bfloat16)] * (n_groups * cuts),
            in_specs=[pl.BlockSpec(memory_space=pltpu.SMEM)] + [hbm] * 3,
            out_specs=[hbm] * n_groups + [pl.BlockSpec(memory_space=pltpu.VMEM)] * (n_groups * cuts),
            scratch_shapes=[
                pltpu.VMEM((n_groups, *block), jnp.bfloat16),
                pltpu.VMEM((ch_dev, span), jnp.float32),
                pltpu.VMEM((n_groups, *block), jnp.bfloat16),
                pltpu.VMEM(block, jnp.float32),
                pltpu.SemaphoreType.DMA((n_groups,)),
                pltpu.SemaphoreType.DMA((2,)),
                pltpu.SemaphoreType.DMA((n_groups,)),
            ],
            name="norm",
        )
        other = flip(scale, 1)
        outs = norm(panel_offset, scale, other, spectra)
        normed += outs[:n_groups]
        outs = outs[n_groups:]
        for g in range(n_groups):
            own[0] += outs[g * cuts : g * cuts + SUBS]
            own[1] += outs[g * cuts + SUBS : (g + 1) * cuts]

    n_chunks = groups * SUBS
    single, n_sends, n_steps = plan(n_chan, n_chunks)
    got = [[], []]
    rest = [own[half][c] for c in range(single, n_chunks) for half in range(2)]
    sends = [own[half][:single] + rest for half in range(2)]

    marks = {LAG: lax.optimization_barrier(is_me)}
    for t in range(LAG + 1, n_sends):
        marks[t] = lax.optimization_barrier(marks[t - 1] * marks[t - 1])
    for t in range(n_steps):
        if t < LAG:
            value = [sends[half][t] for half in range(2)]
        elif t < n_sends:
            mask, *args = lax.optimization_barrier(
                (marks[t], sends[0][t], sends[1][t], got[0][t - LAG], got[1][t - LAG])
            )
            value = [jnp.where(mask > 0, args[half], args[2 + half]) for half in range(2)]
        else:
            value = [got[half][t - LAG] for half in range(2)]
        for half in range(2):
            step = 1 if half == 0 else -1
            pairs = [(ring[i], ring[(i + step) % n_chan]) for i in range(n_chan)]
            got[half].append(lax.ppermute(value[half], "chan", pairs))

    block = (1, f_dev, parts, ch_dev, PANEL)
    return pl.pallas_call(
        functools.partial(cross_kernel, groups, n_chan, n_chunks, n_steps, single, windows ** (-0.5)),
        grid=(NPANEL,),
        out_shape=jax.ShapeDtypeStruct((NPANEL, f_dev, parts, ch_dev, PANEL), jnp.bfloat16),
        in_specs=[pl.BlockSpec(memory_space=pltpu.SMEM)]
        + [hbm] * (groups + 2 * n_chunks + 2 * n_steps),
        out_specs=pl.BlockSpec(block, lambda p: (p, 0, 0, 0, 0)),
        scratch_shapes=[
            pltpu.VMEM((2, f_dev, parts, groups, PANEL, LANES), jnp.bfloat16),
            pltpu.VMEM((groups, f_dev, parts, ch_dev, LANES), jnp.bfloat16),
            pltpu.SemaphoreType.DMA((2,)),
            pltpu.SemaphoreType.DMA((groups,)),
        ],
        name="cross",
    )(panel_block, *normed, *own[0], *own[1], *got[0], *got[1])


def solution(mesh):
    placed = (P("band", None, "chan", None), P(), P(), P())
    return jax.shard_map(
        local,
        mesh=mesh,
        in_specs=placed,
        out_specs=P(None, "band", None, "chan", None),
        check_vma=False,
    )
```

```python
import functools

import jax
import jax.numpy as jnp
from jax import lax
from jax.experimental import pallas as pl
from jax.experimental.pallas import tpu as pltpu
from jax.sharding import PartitionSpec as P


PANEL = 256
NPANEL = 4
HALO = 32
HALF = PANEL // 2
LANES = 128
LAG = 2
SUBS = 4
SPANS = (1, 3)


def spans_of(groups):
    counts = SPANS if sum(SPANS) == groups else (groups,)
    return [(sum(counts[:i]), n) for i, n in enumerate(counts)]


def plan(n_chan, n_chunks):
    both = min(LAG * (n_chan // 2 - 1) // 2, n_chunks)
    single = n_chunks - both
    n_sends = single + 2 * both
    return single, n_sends, max(single + LAG * (n_chan - 2), n_sends + LAG * (n_chan // 2 - 1))


def scale_kernel(channels, bins, p_ref, q_ref, edge_ref, w_ref, scale_ref, s_ref, t_ref):
    rows, _ = scale_ref.shape
    ext = rows + 2 * HALO
    far = lax.rem(lax.axis_index("band"), 2)
    width = w_ref[...]
    span = 2 * width + 1
    inner = p_ref[...] + q_ref[...]
    edge = edge_ref[...]

    @pl.when(far == 0)
    def _():
        s_ref[:HALO, :] = edge
        s_ref[HALO:ext, :] = inner

    @pl.when(far == 1)
    def _():
        s_ref[: ext - HALO, :] = inner
        s_ref[ext - HALO : ext, :] = edge

    s_ref[ext:, :] = jnp.zeros((s_ref.shape[0] - ext, s_ref.shape[1]), jnp.float32)
    t_ref[...] = s_ref[...]
    step = 1
    while step * 2 <= 2 * HALO + 1:
        doubled = s_ref[0:ext, :] + s_ref[step : step + ext, :]
        s_ref[0:ext, :] = doubled
        step *= 2
        here = t_ref[0:ext, :]
        t_ref[0:ext, :] = jnp.where((span & step) != 0, doubled + t_ref[step : step + ext, :], here)
    skip = HALO - width
    step = 1
    n = ext
    while step < HALO:
        n = n - step
        t_ref[0:n, :] = jnp.where((skip & step) != 0, t_ref[step : step + n, :], t_ref[0:n, :])
        step *= 2
    total = t_ref[:rows, :]
    chan = lax.broadcasted_iota(jnp.int32, scale_ref.shape, 0) + (2 * lax.axis_index("chan") + far) * rows
    count = jnp.minimum(chan + width, channels - 1) - jnp.maximum(chan - width, 0) + 1
    scale_ref[...] = lax.rsqrt(total / (count.astype(jnp.float32) * bins) + 1e-06)


def norm_kernel(base, groups, subs, starts_ref, mine_ref, other_ref, x_ref, *rest):
    per = 2 * subs
    normed, own = rest[:groups], rest[groups : groups * (1 + per)]
    x_buf, scale_buf, n_ref, in_sem, scale_sem = rest[groups * (1 + per) :]
    _, f_dev, parts, rows, _ = x_buf.shape
    half_rows = rows // 2
    far = lax.rem(lax.axis_index("band"), 2)
    reads = []
    for g in range(groups):
        lanes = pl.ds((base + g) * LANES, LANES)
        reads.append(pltpu.make_async_copy(x_ref.at[:, :, :, lanes], x_buf.at[g], in_sem.at[g]))
        reads[g].start()
    shares = []
    for i, ref in enumerate((mine_ref, other_ref)):
        at = far * half_rows if i == 0 else (1 - far) * half_rows
        at = pl.ds(pl.multiple_of(at, half_rows), half_rows)
        shares.append(pltpu.make_async_copy(ref, scale_buf.at[at, :], scale_sem.at[i]))
        shares[i].start()
    for copy in shares:
        copy.wait()
    size = HALF // subs
    for g in range(groups):
        reads[g].wait()
        scale = scale_buf[:, g * LANES : (g + 1) * LANES]
        for f in range(f_dev):
            for k in range(parts):
                value = (x_buf[g, f, k].astype(jnp.float32) * scale).astype(jnp.bfloat16)
                normed[g][f, k] = value
                n_ref[f, k] = value.astype(jnp.float32)
        for p in range(NPANEL):
            start = starts_ref[p]
            for i in range(per):
                at = pl.ds(start + i * size, size)
                for f in range(f_dev):
                    for k in range(parts):
                        own[g * per + i][p, f, k] = n_ref[f, k, at, :].astype(jnp.bfloat16)


def cross_kernel(groups, n_chan, n_chunks, n_steps, single, scaling, block_ref, *refs):
    normed, refs = refs[:groups], refs[groups:]
    lists = []
    for size in (n_chunks, n_chunks, n_steps, n_steps):
        lists.append(refs[:size])
        refs = refs[size:]
    (out_ref,) = refs
    per = n_chunks // groups
    panel = pl.program_id(0)

    def place(c):
        return jnp.where(lax.rem(c, 2) == 0, c // 2, n_chan - 1 - c // 2)

    def source(d, half, c):
        if d == 0:
            return lists[half][c]
        if c < single:
            return lists[2 + half][c + LAG * ((d if half == 0 else n_chan - d) - 1)]
        t = single + 2 * (c - single) + half
        way = 0 if d <= n_chan // 2 else 1
        return lists[2 + way][t + LAG * ((d if way == 0 else n_chan - d) - 1)]

    def dot(a, b):
        return lax.dot_general(a, b, (((1,), (1,)), ((), ())), preferred_element_type=jnp.float32)

    ahead = lax.rem(place(lax.axis_index("chan")) - place(block_ref[panel]) + n_chan, n_chan)
    for d in range(n_chan):

        @pl.when(ahead == d)
        def _():
            for f in range(out_ref.shape[1]):
                left = [[n[f, k] for n in normed] for k in range(2)]
                right = jnp.concatenate(
                    [
                        jnp.concatenate(
                            [source(d, half, g * per + j)[panel, f, k] for half in range(2) for j in range(per)], axis=0
                        )
                        for k in range(2)
                        for g in range(groups)
                    ],
                    axis=1,
                )
                real = dot(jnp.concatenate(left[0] + left[1], axis=1), right)
                out_ref[0, f, 0] = (real * scaling).astype(jnp.bfloat16)
                imag = dot(jnp.concatenate(left[1] + [-n for n in left[0]], axis=1), right)
                out_ref[0, f, 1] = (imag * scaling).astype(jnp.bfloat16)


def local(spectra, half_width, panel_block, panel_offset):
    f_dev, parts, ch_dev, windows = spectra.shape
    n_chan, n_band = lax.axis_size("chan"), lax.axis_size("band")
    bins, channels = f_dev * n_band, ch_dev * n_chan
    groups = windows // LANES
    me = lax.axis_index("chan")
    hbm = pl.BlockSpec(memory_space=pl.ANY)
    vmem = pl.BlockSpec(memory_space=pltpu.VMEM)

    ring = list(range(0, n_chan, 2)) + list(range(1, n_chan, 2))[::-1]

    is_me = jnp.broadcast_to((panel_block == me)[:, None, None, None, None], (NPANEL, 1, 1, 1, LANES))
    is_me = is_me.astype(jnp.float32)

    half_rows = ch_dev // 2
    keep_rows = half_rows + HALO
    band = lax.axis_index("band")
    near = band % 2 == 0

    def flip(block, bit):
        return lax.ppermute(block, "band", [(b, b ^ bit) for b in range(n_band)])

    def outward(block):
        pairs = [
            (c * n_band + b, (c + (2 * (b % 2) - 1)) * n_band + (b ^ 1))
            for c in range(n_chan)
            for b in range(n_band)
            if 0 <= c + (2 * (b % 2) - 1) < n_chan
        ]
        return lax.ppermute(block, ("chan", "band"), pairs)

    power = jnp.sum(jnp.square(spectra.astype(jnp.float32)), axis=(0, 1))
    first, second = power[:keep_rows], power[half_rows - HALO :]
    share = jnp.where(near, first, second) + flip(jnp.where(near, second, first), 1)
    bit = 2
    while bit * 2 < n_band:
        share = share + flip(share, bit)
        bit *= 2
    spans = spans_of(groups)
    shares = [share[:, base * LANES : (base + n) * LANES] for base, n in spans]
    theirs = []
    for i in range(len(spans)):
        theirs.append(flip(shares[i], bit))
    edge = jnp.where(near, share[:HALO], share[keep_rows - HALO :])
    edge = edge + flip(edge, bit)
    halo = outward(edge)
    widths = half_width.reshape(1, windows)

    piece = (NPANEL, f_dev, parts, HALF // SUBS, LANES)
    block = (f_dev, parts, ch_dev, LANES)
    cuts = 2 * SUBS
    normed, own = [], [[], []]
    for i, (base, n_groups) in enumerate(spans):
        span = n_groups * LANES
        scale = pl.pallas_call(
            functools.partial(scale_kernel, channels, bins),
            grid=(n_groups,),
            out_shape=jax.ShapeDtypeStruct((half_rows, span), jnp.float32),
            in_specs=[pl.BlockSpec((keep_rows, LANES), lambda g: (0, g))] * 2
            + [pl.BlockSpec((HALO, LANES), lambda g, base=base: (0, base + g))]
            + [pl.BlockSpec((1, LANES), lambda g, base=base: (0, base + g))],
            out_specs=pl.BlockSpec((half_rows, LANES), lambda g: (0, g)),
            scratch_shapes=[pltpu.VMEM((half_rows + 4 * HALO, LANES), jnp.float32)] * 2,
            compiler_params=pltpu.CompilerParams(vmem_limit_bytes=6 << 20),
            name="scale",
        )
        scale = scale(shares[i], theirs[i], halo, widths)
        norm = pl.pallas_call(
            functools.partial(norm_kernel, base, n_groups, SUBS),
            out_shape=[pltpu.VMEM(block, jnp.bfloat16)] * n_groups
            + [pltpu.VMEM(piece, jnp.bfloat16)] * (n_groups * cuts),
            in_specs=[pl.BlockSpec(memory_space=pltpu.SMEM)] + [hbm] * 3,
            out_specs=[vmem] * (n_groups * (1 + cuts)),
            scratch_shapes=[
                pltpu.VMEM((n_groups, *block), jnp.bfloat16),
                pltpu.VMEM((ch_dev, span), jnp.float32),
                pltpu.VMEM(block, jnp.float32),
                pltpu.SemaphoreType.DMA((n_groups,)),
                pltpu.SemaphoreType.DMA((2,)),
            ],
            compiler_params=pltpu.CompilerParams(vmem_limit_bytes=16 << 20),
            name="norm",
        )
        other = flip(scale, 1)
        outs = norm(panel_offset, scale, other, spectra)
        normed += outs[:n_groups]
        outs = outs[n_groups:]
        for g in range(n_groups):
            own[0] += outs[g * cuts : g * cuts + SUBS]
            own[1] += outs[g * cuts + SUBS : (g + 1) * cuts]

    n_chunks = groups * SUBS
    single, n_sends, n_steps = plan(n_chan, n_chunks)
    got = [[], []]
    rest = [own[half][c] for c in range(single, n_chunks) for half in range(2)]
    sends = [own[half][:single] + rest for half in range(2)]

    marks = {LAG: [lax.optimization_barrier(is_me), lax.optimization_barrier(is_me + is_me)]}
    for t in range(LAG + 1, n_sends):
        marks[t] = []
        for half in range(2):
            marks[t].append(lax.optimization_barrier(jnp.minimum(marks[t - 1][half], 2.0 - half)))
    for t in range(n_steps):
        for half in range(2):
            value = sends[half][t] if t < n_sends else got[half][t - LAG]
            if LAG <= t < n_sends:
                mask, mine, back = lax.optimization_barrier((marks[t][half], value, got[half][t - LAG]))
                value = jnp.where(mask > 0, mine, back)
            step = 1 if half == 0 else -1
            pairs = [(ring[i], ring[(i + step) % n_chan]) for i in range(n_chan)]
            got[half].append(lax.ppermute(value, "chan", pairs))

    block = (1, f_dev, parts, ch_dev, PANEL)
    return pl.pallas_call(
        functools.partial(cross_kernel, groups, n_chan, n_chunks, n_steps, single, windows ** (-0.5)),
        grid=(NPANEL,),
        out_shape=jax.ShapeDtypeStruct((NPANEL, f_dev, parts, ch_dev, PANEL), jnp.bfloat16),
        in_specs=[pl.BlockSpec(memory_space=pltpu.SMEM)]
        + [vmem] * (groups + 2 * n_chunks + 2 * n_steps),
        out_specs=pl.BlockSpec(block, lambda p: (p, 0, 0, 0, 0)),
        compiler_params=pltpu.CompilerParams(vmem_limit_bytes=20 << 20),
        name="cross",
    )(panel_block, *normed, *own[0], *own[1], *got[0], *got[1])


def solution(mesh):
    placed = (P("band", None, "chan", None), P(), P(), P())
    return jax.shard_map(
        local,
        mesh=mesh,
        in_specs=placed,
        out_specs=P(None, "band", None, "chan", None),
        check_vma=False,
    )
```

```python
import functools

import jax
import jax.numpy as jnp
from jax import lax
from jax.experimental import pallas as pl
from jax.experimental.pallas import tpu as pltpu
from jax.sharding import PartitionSpec as P


PANEL = 256
NPANEL = 4
HALO = 32
HALF = PANEL // 2
LANES = 128
LAG = 2
SUBS = 4
SPANS = (1, 1, 2)


def spans_of(groups):
    counts = SPANS if sum(SPANS) == groups else (groups,)
    return [(sum(counts[:i]), n) for i, n in enumerate(counts)]


def plan(n_chan, n_chunks):
    both = min(LAG * (n_chan // 2 - 1) // 2, n_chunks)
    single = n_chunks - both
    n_sends = single + 2 * both
    return single, n_sends, max(single + LAG * (n_chan - 2), n_sends + LAG * (n_chan // 2 - 1))


def scale_kernel(channels, bins, p_ref, q_ref, edge_ref, w_ref, scale_ref, s_ref, t_ref):
    rows, _ = scale_ref.shape
    ext = rows + 2 * HALO
    far = lax.rem(lax.axis_index("band"), 2)
    width = w_ref[...]
    span = 2 * width + 1
    inner = p_ref[...] + q_ref[...]
    edge = edge_ref[...]

    @pl.when(far == 0)
    def _():
        s_ref[:HALO, :] = edge
        s_ref[HALO:ext, :] = inner

    @pl.when(far == 1)
    def _():
        s_ref[: ext - HALO, :] = inner
        s_ref[ext - HALO : ext, :] = edge

    s_ref[ext:, :] = jnp.zeros((s_ref.shape[0] - ext, s_ref.shape[1]), jnp.float32)
    t_ref[...] = s_ref[...]
    step = 1
    while step * 2 <= 2 * HALO + 1:
        doubled = s_ref[0:ext, :] + s_ref[step : step + ext, :]
        s_ref[0:ext, :] = doubled
        step *= 2
        here = t_ref[0:ext, :]
        t_ref[0:ext, :] = jnp.where((span & step) != 0, doubled + t_ref[step : step + ext, :], here)
    skip = HALO - width
    step = 1
    n = ext
    while step < HALO:
        n = n - step
        t_ref[0:n, :] = jnp.where((skip & step) != 0, t_ref[step : step + n, :], t_ref[0:n, :])
        step *= 2
    total = t_ref[:rows, :]
    chan = lax.broadcasted_iota(jnp.int32, scale_ref.shape, 0) + (2 * lax.axis_index("chan") + far) * rows
    count = jnp.minimum(chan + width, channels - 1) - jnp.maximum(chan - width, 0) + 1
    scale_ref[...] = lax.rsqrt(total / (count.astype(jnp.float32) * bins) + 1e-06)


def norm_kernel(base, groups, subs, starts_ref, mine_ref, other_ref, x_ref, *rest):
    per = 2 * subs
    normed, own = rest[:groups], rest[groups : groups * (1 + per)]
    x_buf, scale_buf, n_ref, in_sem, scale_sem = rest[groups * (1 + per) :]
    _, f_dev, parts, rows, _ = x_buf.shape
    half_rows = rows // 2
    far = lax.rem(lax.axis_index("band"), 2)
    reads = []
    for g in range(groups):
        lanes = pl.ds((base + g) * LANES, LANES)
        reads.append(pltpu.make_async_copy(x_ref.at[:, :, :, lanes], x_buf.at[g], in_sem.at[g]))
        reads[g].start()
    shares = []
    for i, ref in enumerate((mine_ref, other_ref)):
        at = far * half_rows if i == 0 else (1 - far) * half_rows
        at = pl.ds(pl.multiple_of(at, half_rows), half_rows)
        shares.append(pltpu.make_async_copy(ref, scale_buf.at[at, :], scale_sem.at[i]))
        shares[i].start()
    for copy in shares:
        copy.wait()
    size = HALF // subs
    for g in range(groups):
        reads[g].wait()
        scale = scale_buf[:, g * LANES : (g + 1) * LANES]
        for f in range(f_dev):
            for k in range(parts):
                value = (x_buf[g, f, k].astype(jnp.float32) * scale).astype(jnp.bfloat16)
                normed[g][f, k] = value
                n_ref[f, k] = value.astype(jnp.float32)
        for p in range(NPANEL):
            start = starts_ref[p]
            for i in range(per):
                at = pl.ds(start + i * size, size)
                for f in range(f_dev):
                    for k in range(parts):
                        own[g * per + i][p, f, k] = n_ref[f, k, at, :].astype(jnp.bfloat16)


def cross_kernel(groups, n_chan, n_chunks, n_steps, single, scaling, block_ref, *refs):
    normed, refs = refs[:groups], refs[groups:]
    lists = []
    for size in (n_chunks, n_chunks, n_steps, n_steps):
        lists.append(refs[:size])
        refs = refs[size:]
    (out_ref,) = refs
    per = n_chunks // groups
    panel = pl.program_id(0)

    def place(c):
        return jnp.where(lax.rem(c, 2) == 0, c // 2, n_chan - 1 - c // 2)

    def source(d, half, c):
        if d == 0:
            return lists[half][c]
        if c < single:
            return lists[2 + half][c + LAG * ((d if half == 0 else n_chan - d) - 1)]
        t = single + 2 * (c - single) + half
        way = 0 if d <= n_chan // 2 else 1
        return lists[2 + way][t + LAG * ((d if way == 0 else n_chan - d) - 1)]

    def dot(a, b):
        return lax.dot_general(a, b, (((1,), (1,)), ((), ())), preferred_element_type=jnp.float32)

    ahead = lax.rem(place(lax.axis_index("chan")) - place(block_ref[panel]) + n_chan, n_chan)
    for d in range(n_chan):

        @pl.when(ahead == d)
        def _():
            for f in range(out_ref.shape[1]):
                left = [[n[f, k] for n in normed] for k in range(2)]
                right = jnp.concatenate(
                    [
                        jnp.concatenate(
                            [source(d, half, g * per + j)[panel, f, k] for half in range(2) for j in range(per)], axis=0
                        )
                        for k in range(2)
                        for g in range(groups)
                    ],
                    axis=1,
                )
                real = dot(jnp.concatenate(left[0] + left[1], axis=1), right)
                out_ref[0, f, 0] = (real * scaling).astype(jnp.bfloat16)
                imag = dot(jnp.concatenate(left[1] + [-n for n in left[0]], axis=1), right)
                out_ref[0, f, 1] = (imag * scaling).astype(jnp.bfloat16)


def local(spectra, half_width, panel_block, panel_offset):
    f_dev, parts, ch_dev, windows = spectra.shape
    n_chan, n_band = lax.axis_size("chan"), lax.axis_size("band")
    bins, channels = f_dev * n_band, ch_dev * n_chan
    groups = windows // LANES
    me = lax.axis_index("chan")
    hbm = pl.BlockSpec(memory_space=pl.ANY)
    vmem = pl.BlockSpec(memory_space=pltpu.VMEM)

    ring = list(range(0, n_chan, 2)) + list(range(1, n_chan, 2))[::-1]

    is_me = jnp.broadcast_to((panel_block == me)[:, None, None, None, None], (NPANEL, 1, 1, 1, LANES))
    is_me = is_me.astype(jnp.float32)

    half_rows = ch_dev // 2
    keep_rows = half_rows + HALO
    band = lax.axis_index("band")
    near = band % 2 == 0

    def flip(block, bit):
        return lax.ppermute(block, "band", [(b, b ^ bit) for b in range(n_band)])

    def outward(block):
        pairs = [
            (c * n_band + b, (c + (2 * (b % 2) - 1)) * n_band + (b ^ 1))
            for c in range(n_chan)
            for b in range(n_band)
            if 0 <= c + (2 * (b % 2) - 1) < n_chan
        ]
        return lax.ppermute(block, ("chan", "band"), pairs)

    def power_of(block):
        return jnp.sum(jnp.square(block.astype(jnp.float32)), axis=(0, 1))

    low, high = power_of(spectra[:, :, :HALO]), power_of(spectra[:, :, ch_dev - HALO :])
    edge = jnp.where(near, low, high) + flip(jnp.where(near, high, low), 1)
    power = power_of(spectra)
    first, second = power[:keep_rows], power[half_rows - HALO :]
    share = jnp.where(near, first, second) + flip(jnp.where(near, second, first), 1)
    bit = 2
    while bit * 2 < n_band:
        edge = edge + flip(edge, bit)
        share = share + flip(share, bit)
        bit *= 2
    edge = edge + flip(edge, bit)
    halo = outward(edge)
    spans = spans_of(groups)
    shares = [share[:, base * LANES : (base + n) * LANES] for base, n in spans]
    theirs = []
    for i in range(len(spans)):
        theirs.append(flip(shares[i], bit))
    widths = half_width.reshape(1, windows)

    piece = (NPANEL, f_dev, parts, HALF // SUBS, LANES)
    block = (f_dev, parts, ch_dev, LANES)
    cuts = 2 * SUBS
    normed, own = [], [[], []]
    for i, (base, n_groups) in enumerate(spans):
        span = n_groups * LANES
        scale = pl.pallas_call(
            functools.partial(scale_kernel, channels, bins),
            grid=(n_groups,),
            out_shape=jax.ShapeDtypeStruct((half_rows, span), jnp.float32),
            in_specs=[pl.BlockSpec((keep_rows, LANES), lambda g: (0, g))] * 2
            + [pl.BlockSpec((HALO, LANES), lambda g, base=base: (0, base + g))]
            + [pl.BlockSpec((1, LANES), lambda g, base=base: (0, base + g))],
            out_specs=pl.BlockSpec((half_rows, LANES), lambda g: (0, g)),
            scratch_shapes=[pltpu.VMEM((half_rows + 4 * HALO, LANES), jnp.float32)] * 2,
            compiler_params=pltpu.CompilerParams(vmem_limit_bytes=6 << 20),
            name="scale",
        )
        scale = scale(shares[i], theirs[i], halo, widths)
        norm = pl.pallas_call(
            functools.partial(norm_kernel, base, n_groups, SUBS),
            out_shape=[pltpu.VMEM(block, jnp.bfloat16)] * n_groups
            + [pltpu.VMEM(piece, jnp.bfloat16)] * (n_groups * cuts),
            in_specs=[pl.BlockSpec(memory_space=pltpu.SMEM)] + [hbm] * 3,
            out_specs=[vmem] * (n_groups * (1 + cuts)),
            scratch_shapes=[
                pltpu.VMEM((n_groups, *block), jnp.bfloat16),
                pltpu.VMEM((ch_dev, span), jnp.float32),
                pltpu.VMEM(block, jnp.float32),
                pltpu.SemaphoreType.DMA((n_groups,)),
                pltpu.SemaphoreType.DMA((2,)),
            ],
            compiler_params=pltpu.CompilerParams(vmem_limit_bytes=16 << 20),
            name="norm",
        )
        other = flip(scale, 1)
        outs = norm(panel_offset, scale, other, spectra)
        normed += outs[:n_groups]
        outs = outs[n_groups:]
        for g in range(n_groups):
            own[0] += outs[g * cuts : g * cuts + SUBS]
            own[1] += outs[g * cuts + SUBS : (g + 1) * cuts]

    n_chunks = groups * SUBS
    single, n_sends, n_steps = plan(n_chan, n_chunks)
    got = [[], []]
    rest = [own[half][c] for c in range(single, n_chunks) for half in range(2)]
    sends = [own[half][:single] + rest for half in range(2)]

    marks = {LAG: [lax.optimization_barrier(is_me), lax.optimization_barrier(is_me + is_me)]}
    for t in range(LAG + 1, n_sends):
        marks[t] = []
        for half in range(2):
            marks[t].append(lax.optimization_barrier(jnp.minimum(marks[t - 1][half], 2.0 - half)))
    for t in range(n_steps):
        for half in range(2):
            value = sends[half][t] if t < n_sends else got[half][t - LAG]
            if LAG <= t < n_sends:
                mask, mine, back = lax.optimization_barrier((marks[t][half], value, got[half][t - LAG]))
                value = jnp.where(mask > 0, mine, back)
            step = 1 if half == 0 else -1
            pairs = [(ring[i], ring[(i + step) % n_chan]) for i in range(n_chan)]
            got[half].append(lax.ppermute(value, "chan", pairs))

    block = (1, f_dev, parts, ch_dev, PANEL)
    return pl.pallas_call(
        functools.partial(cross_kernel, groups, n_chan, n_chunks, n_steps, single, windows ** (-0.5)),
        grid=(NPANEL,),
        out_shape=jax.ShapeDtypeStruct((NPANEL, f_dev, parts, ch_dev, PANEL), jnp.bfloat16),
        in_specs=[pl.BlockSpec(memory_space=pltpu.SMEM)]
        + [vmem] * (groups + 2 * n_chunks + 2 * n_steps),
        out_specs=pl.BlockSpec(block, lambda p: (p, 0, 0, 0, 0)),
        compiler_params=pltpu.CompilerParams(vmem_limit_bytes=20 << 20),
        name="cross",
    )(panel_block, *normed, *own[0], *own[1], *got[0], *got[1])


def solution(mesh):
    placed = (P("band", None, "chan", None), P(), P(), P())
    return jax.shard_map(
        local,
        mesh=mesh,
        in_specs=placed,
        out_specs=P(None, "band", None, "chan", None),
        check_vma=False,
    )
```

```python
import functools

import jax
import jax.numpy as jnp
from jax import lax
from jax.experimental import pallas as pl
from jax.experimental.pallas import tpu as pltpu
from jax.sharding import PartitionSpec as P


PANEL = 256
NPANEL = 4
HALO = 32
HALF = PANEL // 2
LANES = 128
LAG = 2
SUBS = 4
SPANS = (1, 1, 2)


def spans_of(groups):
    counts = SPANS if sum(SPANS) == groups else (groups,)
    return [(sum(counts[:i]), n) for i, n in enumerate(counts)]


def plan(n_chan, n_chunks):
    both = min(LAG * (n_chan // 2 - 1) // 2, n_chunks)
    single = n_chunks - both
    n_sends = single + 2 * both
    return single, n_sends, max(single + LAG * (n_chan - 2), n_sends + LAG * (n_chan // 2 - 1))


def early_groups(n_chan, groups):
    single, _, n_steps = plan(n_chan, groups * SUBS)
    whole = min(single, n_steps - 2 - LAG * (n_chan - 2))
    return min(max(whole, 0) // SUBS, groups - 1)


def scale_kernel(channels, bins, p_ref, q_ref, edge_ref, w_ref, scale_ref, s_ref, t_ref):
    rows, _ = scale_ref.shape
    ext = rows + 2 * HALO
    far = lax.rem(lax.axis_index("band"), 2)
    width = w_ref[...]
    span = 2 * width + 1
    inner = p_ref[...] + q_ref[...]
    edge = edge_ref[...]

    @pl.when(far == 0)
    def _():
        s_ref[:HALO, :] = edge
        s_ref[HALO:ext, :] = inner

    @pl.when(far == 1)
    def _():
        s_ref[: ext - HALO, :] = inner
        s_ref[ext - HALO : ext, :] = edge

    s_ref[ext:, :] = jnp.zeros((s_ref.shape[0] - ext, s_ref.shape[1]), jnp.float32)
    t_ref[...] = s_ref[...]
    step = 1
    while step * 2 <= 2 * HALO + 1:
        doubled = s_ref[0:ext, :] + s_ref[step : step + ext, :]
        s_ref[0:ext, :] = doubled
        step *= 2
        here = t_ref[0:ext, :]
        t_ref[0:ext, :] = jnp.where((span & step) != 0, doubled + t_ref[step : step + ext, :], here)
    skip = HALO - width
    step = 1
    n = ext
    while step < HALO:
        n = n - step
        t_ref[0:n, :] = jnp.where((skip & step) != 0, t_ref[step : step + n, :], t_ref[0:n, :])
        step *= 2
    total = t_ref[:rows, :]
    chan = lax.broadcasted_iota(jnp.int32, scale_ref.shape, 0) + (2 * lax.axis_index("chan") + far) * rows
    count = jnp.minimum(chan + width, channels - 1) - jnp.maximum(chan - width, 0) + 1
    scale_ref[...] = lax.rsqrt(total / (count.astype(jnp.float32) * bins) + 1e-06)


def norm_kernel(base, groups, subs, starts_ref, mine_ref, other_ref, x_ref, *rest):
    per = 2 * subs
    normed, own = rest[:groups], rest[groups : groups * (1 + per)]
    x_buf, scale_buf, n_ref, in_sem, scale_sem = rest[groups * (1 + per) :]
    _, f_dev, parts, rows, _ = x_buf.shape
    half_rows = rows // 2
    far = lax.rem(lax.axis_index("band"), 2)
    reads = []
    for g in range(groups):
        lanes = pl.ds((base + g) * LANES, LANES)
        reads.append(pltpu.make_async_copy(x_ref.at[:, :, :, lanes], x_buf.at[g], in_sem.at[g]))
        reads[g].start()
    shares = []
    for i, ref in enumerate((mine_ref, other_ref)):
        at = far * half_rows if i == 0 else (1 - far) * half_rows
        at = pl.ds(pl.multiple_of(at, half_rows), half_rows)
        shares.append(pltpu.make_async_copy(ref, scale_buf.at[at, :], scale_sem.at[i]))
        shares[i].start()
    for copy in shares:
        copy.wait()
    size = HALF // subs
    for g in range(groups):
        reads[g].wait()
        scale = scale_buf[:, g * LANES : (g + 1) * LANES]
        for f in range(f_dev):
            for k in range(parts):
                value = (x_buf[g, f, k].astype(jnp.float32) * scale).astype(jnp.bfloat16)
                normed[g][f, k] = value
                n_ref[f, k] = value.astype(jnp.float32)
        for p in range(NPANEL):
            start = starts_ref[p]
            for i in range(per):
                at = pl.ds(start + i * size, size)
                for f in range(f_dev):
                    for k in range(parts):
                        own[g * per + i][p, f, k] = n_ref[f, k, at, :].astype(jnp.bfloat16)


def cross_kernel(base, groups, n_chan, n_chunks, n_steps, single, scaling, block_ref, *refs):
    normed, refs = refs[:groups], refs[groups:]
    lists = []
    for size in (n_chunks, n_chunks, n_steps, n_steps):
        lists.append(refs[:size])
        refs = refs[size:]
    out_ref = refs[-1]
    per = SUBS
    panel = pl.program_id(0)

    def store(f, part, value):
        if scaling is None:
            out_ref[panel, f, part] = value
            return
        if len(refs) > 1:
            value = value + refs[0][panel, f, part]
        out_ref[0, f, part] = (value * scaling).astype(jnp.bfloat16)

    def place(c):
        return jnp.where(lax.rem(c, 2) == 0, c // 2, n_chan - 1 - c // 2)

    def source(d, half, c):
        if d == 0:
            return lists[half][c]
        if c < single:
            return lists[2 + half][c + LAG * ((d if half == 0 else n_chan - d) - 1)]
        t = single + 2 * (c - single) + half
        way = 0 if d <= n_chan // 2 else 1
        return lists[2 + way][t + LAG * ((d if way == 0 else n_chan - d) - 1)]

    def dot(a, b):
        return lax.dot_general(a, b, (((1,), (1,)), ((), ())), preferred_element_type=jnp.float32)

    ahead = lax.rem(place(lax.axis_index("chan")) - place(block_ref[panel]) + n_chan, n_chan)
    for d in range(n_chan):

        @pl.when(ahead == d)
        def _():
            for f in range(out_ref.shape[1]):
                left = [[n[f, k] for n in normed] for k in range(2)]
                right = jnp.concatenate(
                    [
                        jnp.concatenate(
                            [source(d, half, (base + g) * per + j)[panel, f, k] for half in range(2) for j in range(per)], axis=0
                        )
                        for k in range(2)
                        for g in range(groups)
                    ],
                    axis=1,
                )
                real = dot(jnp.concatenate(left[0] + left[1], axis=1), right)
                store(f, 0, real)
                imag = dot(jnp.concatenate(left[1] + [-n for n in left[0]], axis=1), right)
                store(f, 1, imag)


def local(spectra, half_width, panel_block, panel_offset):
    f_dev, parts, ch_dev, windows = spectra.shape
    n_chan, n_band = lax.axis_size("chan"), lax.axis_size("band")
    bins, channels = f_dev * n_band, ch_dev * n_chan
    groups = windows // LANES
    me = lax.axis_index("chan")
    hbm = pl.BlockSpec(memory_space=pl.ANY)
    vmem = pl.BlockSpec(memory_space=pltpu.VMEM)

    ring = list(range(0, n_chan, 2)) + list(range(1, n_chan, 2))[::-1]

    is_me = jnp.broadcast_to((panel_block == me)[:, None, None, None, None], (NPANEL, 1, 1, 1, LANES))
    is_me = is_me.astype(jnp.float32)

    half_rows = ch_dev // 2
    keep_rows = half_rows + HALO
    band = lax.axis_index("band")
    near = band % 2 == 0

    def flip(block, bit):
        return lax.ppermute(block, "band", [(b, b ^ bit) for b in range(n_band)])

    def outward(block):
        pairs = [
            (c * n_band + b, (c + (2 * (b % 2) - 1)) * n_band + (b ^ 1))
            for c in range(n_chan)
            for b in range(n_band)
            if 0 <= c + (2 * (b % 2) - 1) < n_chan
        ]
        return lax.ppermute(block, ("chan", "band"), pairs)

    def power_of(block):
        return jnp.sum(jnp.square(block.astype(jnp.float32)), axis=(0, 1))

    low, high = power_of(spectra[:, :, :HALO]), power_of(spectra[:, :, ch_dev - HALO :])
    edge = jnp.where(near, low, high) + flip(jnp.where(near, high, low), 1)
    power = power_of(spectra)
    first, second = power[:keep_rows], power[half_rows - HALO :]
    share = jnp.where(near, first, second) + flip(jnp.where(near, second, first), 1)
    bit = 2
    while bit * 2 < n_band:
        edge = edge + flip(edge, bit)
        share = share + flip(share, bit)
        bit *= 2
    edge = edge + flip(edge, bit)
    halo = outward(edge)
    spans = spans_of(groups)
    shares = [share[:, base * LANES : (base + n) * LANES] for base, n in spans]
    theirs = []
    for i in range(len(spans)):
        theirs.append(flip(shares[i], bit))
    widths = half_width.reshape(1, windows)

    piece = (NPANEL, f_dev, parts, HALF // SUBS, LANES)
    block = (f_dev, parts, ch_dev, LANES)
    cuts = 2 * SUBS
    normed, own = [], [[], []]
    for i, (base, n_groups) in enumerate(spans):
        span = n_groups * LANES
        scale = pl.pallas_call(
            functools.partial(scale_kernel, channels, bins),
            grid=(n_groups,),
            out_shape=jax.ShapeDtypeStruct((half_rows, span), jnp.float32),
            in_specs=[pl.BlockSpec((keep_rows, LANES), lambda g: (0, g))] * 2
            + [pl.BlockSpec((HALO, LANES), lambda g, base=base: (0, base + g))]
            + [pl.BlockSpec((1, LANES), lambda g, base=base: (0, base + g))],
            out_specs=pl.BlockSpec((half_rows, LANES), lambda g: (0, g)),
            scratch_shapes=[pltpu.VMEM((half_rows + 4 * HALO, LANES), jnp.float32)] * 2,
            compiler_params=pltpu.CompilerParams(vmem_limit_bytes=6 << 20),
            name="scale",
        )
        scale = scale(shares[i], theirs[i], halo, widths)
        norm = pl.pallas_call(
            functools.partial(norm_kernel, base, n_groups, SUBS),
            out_shape=[pltpu.VMEM(block, jnp.bfloat16)] * n_groups
            + [pltpu.VMEM(piece, jnp.bfloat16)] * (n_groups * cuts),
            in_specs=[pl.BlockSpec(memory_space=pltpu.SMEM)] + [hbm] * 3,
            out_specs=[vmem] * (n_groups * (1 + cuts)),
            scratch_shapes=[
                pltpu.VMEM((n_groups, *block), jnp.bfloat16),
                pltpu.VMEM((ch_dev, span), jnp.float32),
                pltpu.VMEM(block, jnp.float32),
                pltpu.SemaphoreType.DMA((n_groups,)),
                pltpu.SemaphoreType.DMA((2,)),
            ],
            compiler_params=pltpu.CompilerParams(vmem_limit_bytes=16 << 20),
            name="norm",
        )
        other = flip(scale, 1)
        outs = norm(panel_offset, scale, other, spectra)
        normed += outs[:n_groups]
        outs = outs[n_groups:]
        for g in range(n_groups):
            own[0] += outs[g * cuts : g * cuts + SUBS]
            own[1] += outs[g * cuts + SUBS : (g + 1) * cuts]

    n_chunks = groups * SUBS
    single, n_sends, n_steps = plan(n_chan, n_chunks)
    n_ready = early_groups(n_chan, groups) * SUBS + LAG * (n_chan - 2)
    got = [[], []]
    rest = [own[half][c] for c in range(single, n_chunks) for half in range(2)]
    sends = [own[half][:single] + rest for half in range(2)]

    marks = {LAG: [lax.optimization_barrier(is_me), lax.optimization_barrier(is_me + is_me)]}
    for t in range(LAG + 1, n_sends):
        marks[t] = []
        for half in range(2):
            marks[t].append(lax.optimization_barrier(jnp.minimum(marks[t - 1][half], 2.0 - half)))
    for t in range(n_steps):
        for half in range(2):
            value = sends[half][t] if t < n_sends else got[half][t - LAG]
            if LAG <= t < n_sends:
                mask, mine, back = lax.optimization_barrier((marks[t][half], value, got[half][t - LAG]))
                value = jnp.where(mask > 0, mine, back)
            step = 1 if half == 0 else -1
            pairs = [(ring[i], ring[(i + step) % n_chan]) for i in range(n_chan)]
            got[half].append(lax.ppermute(value, "chan", pairs))

    block = (f_dev, parts, ch_dev, PANEL)
    messages = [*own[0], *own[1], *got[0], *got[1]]
    ahead = early_groups(n_chan, groups)
    sums = []
    if ahead:
        early = pl.pallas_call(
            functools.partial(cross_kernel, 0, ahead, n_chan, n_chunks, n_ready, single, None),
            grid=(NPANEL,),
            out_shape=pltpu.VMEM((NPANEL, *block), jnp.float32),
            in_specs=[pl.BlockSpec(memory_space=pltpu.SMEM)] + [vmem] * (ahead + 2 * n_chunks + 2 * n_ready),
            out_specs=vmem,
            compiler_params=pltpu.CompilerParams(vmem_limit_bytes=16 << 20),
            name="early",
        )
        sums = [early(panel_block, *normed[:ahead], *own[0], *own[1], *got[0][:n_ready], *got[1][:n_ready])]
    return pl.pallas_call(
        functools.partial(
            cross_kernel, ahead, groups - ahead, n_chan, n_chunks, n_steps, single, windows ** (-0.5)
        ),
        grid=(NPANEL,),
        out_shape=jax.ShapeDtypeStruct((NPANEL, *block), jnp.bfloat16),
        in_specs=[pl.BlockSpec(memory_space=pltpu.SMEM)] + [vmem] * (groups - ahead + len(messages) + len(sums)),
        out_specs=pl.BlockSpec((1, *block), lambda p: (p, 0, 0, 0, 0)),
        compiler_params=pltpu.CompilerParams(vmem_limit_bytes=20 << 20),
        name="cross",
    )(panel_block, *normed[ahead:], *messages, *sums)


def solution(mesh):
    placed = (P("band", None, "chan", None), P(), P(), P())
    return jax.shard_map(
        local,
        mesh=mesh,
        in_specs=placed,
        out_specs=P(None, "band", None, "chan", None),
        check_vma=False,
    )
```

```python
import functools

import jax
import jax.numpy as jnp
from jax import lax
from jax.experimental import pallas as pl
from jax.experimental.pallas import tpu as pltpu
from jax.sharding import PartitionSpec as P


PANEL = 256
NPANEL = 4
HALO = 32
HALF = PANEL // 2
LANES = 128
LAG = 2
SUBS = 4
SPANS = (1, 1, 1, 1)


def spans_of(groups):
    counts = SPANS if sum(SPANS) == groups else (groups,)
    return [(sum(counts[:i]), n) for i, n in enumerate(counts)]


def plan(n_chan, n_chunks):
    both = min(LAG * (n_chan // 2 - 1) // 2, n_chunks)
    single = n_chunks - both
    n_sends = single + 2 * both
    return single, n_sends, max(single + LAG * (n_chan - 2), n_sends + LAG * (n_chan // 2 - 1))


def early_groups(n_chan, groups):
    single, _, n_steps = plan(n_chan, groups * SUBS)
    whole = min(single, n_steps - 2 - LAG * (n_chan - 2))
    return min(max(whole, 0) // SUBS, groups - 1)


def scale_kernel(channels, bins, p_ref, q_ref, edge_ref, w_ref, scale_ref, s_ref, t_ref):
    rows, _ = scale_ref.shape
    ext = rows + 2 * HALO
    far = lax.rem(lax.axis_index("band"), 2)
    width = w_ref[...]
    span = 2 * width + 1
    inner = p_ref[...] + q_ref[...]
    edge = edge_ref[...]

    @pl.when(far == 0)
    def _():
        s_ref[:HALO, :] = edge
        s_ref[HALO:ext, :] = inner

    @pl.when(far == 1)
    def _():
        s_ref[: ext - HALO, :] = inner
        s_ref[ext - HALO : ext, :] = edge

    s_ref[ext:, :] = jnp.zeros((s_ref.shape[0] - ext, s_ref.shape[1]), jnp.float32)
    t_ref[...] = s_ref[...]
    step = 1
    while step * 2 <= 2 * HALO + 1:
        doubled = s_ref[0:ext, :] + s_ref[step : step + ext, :]
        s_ref[0:ext, :] = doubled
        step *= 2
        here = t_ref[0:ext, :]
        t_ref[0:ext, :] = jnp.where((span & step) != 0, doubled + t_ref[step : step + ext, :], here)
    skip = HALO - width
    step = 1
    n = ext
    while step < HALO:
        n = n - step
        t_ref[0:n, :] = jnp.where((skip & step) != 0, t_ref[step : step + n, :], t_ref[0:n, :])
        step *= 2
    total = t_ref[:rows, :]
    chan = lax.broadcasted_iota(jnp.int32, scale_ref.shape, 0) + (2 * lax.axis_index("chan") + far) * rows
    count = jnp.minimum(chan + width, channels - 1) - jnp.maximum(chan - width, 0) + 1
    scale_ref[...] = lax.rsqrt(total / (count.astype(jnp.float32) * bins) + 1e-06)


def norm_kernel(groups, subs, starts_ref, mine_ref, other_ref, x_ref, *rest):
    per = 2 * subs
    normed, own = rest[:groups], rest[groups : groups * (1 + per)]
    scale_buf, n_ref, scale_sem = rest[groups * (1 + per) :]
    f_dev, parts, rows, _ = x_ref.shape
    half_rows = rows // 2
    far = lax.rem(lax.axis_index("band"), 2)
    shares = []
    for i, ref in enumerate((mine_ref, other_ref)):
        at = far * half_rows if i == 0 else (1 - far) * half_rows
        at = pl.ds(pl.multiple_of(at, half_rows), half_rows)
        shares.append(pltpu.make_async_copy(ref, scale_buf.at[at, :], scale_sem.at[i]))
        shares[i].start()
    for copy in shares:
        copy.wait()
    size = HALF // subs
    for g in range(groups):
        lanes = slice(g * LANES, (g + 1) * LANES)
        scale = scale_buf[:, lanes]
        for f in range(f_dev):
            for k in range(parts):
                value = (x_ref[f, k, :, lanes].astype(jnp.float32) * scale).astype(jnp.bfloat16)
                normed[g][f, k] = value
                n_ref[f, k] = value.astype(jnp.float32)
        for p in range(NPANEL):
            start = starts_ref[p]
            for i in range(per):
                at = pl.ds(start + i * size, size)
                for f in range(f_dev):
                    for k in range(parts):
                        own[g * per + i][p, f, k] = n_ref[f, k, at, :].astype(jnp.bfloat16)


def cross_kernel(base, groups, n_chan, n_chunks, n_steps, single, scaling, block_ref, *refs):
    normed, refs = refs[:groups], refs[groups:]
    lists = []
    for size in (n_chunks, n_chunks, n_steps, n_steps):
        lists.append(refs[:size])
        refs = refs[size:]
    out_ref = refs[-1]
    per = SUBS
    panel = pl.program_id(0)

    def store(f, part, value):
        if scaling is None:
            out_ref[panel, f, part] = value
            return
        if len(refs) > 1:
            value = value + refs[0][panel, f, part]
        out_ref[0, f, part] = (value * scaling).astype(jnp.bfloat16)

    def place(c):
        return jnp.where(lax.rem(c, 2) == 0, c // 2, n_chan - 1 - c // 2)

    def source(d, half, c):
        if d == 0:
            return lists[half][c]
        if c < single:
            return lists[2 + half][c + LAG * ((d if half == 0 else n_chan - d) - 1)]
        t = single + 2 * (c - single) + half
        way = 0 if d <= n_chan // 2 else 1
        return lists[2 + way][t + LAG * ((d if way == 0 else n_chan - d) - 1)]

    def dot(a, b):
        return lax.dot_general(a, b, (((1,), (1,)), ((), ())), preferred_element_type=jnp.float32)

    ahead = lax.rem(place(lax.axis_index("chan")) - place(block_ref[panel]) + n_chan, n_chan)
    for d in range(n_chan):

        @pl.when(ahead == d)
        def _():
            for f in range(out_ref.shape[1]):
                left = [[n[f, k] for n in normed] for k in range(2)]
                right = jnp.concatenate(
                    [
                        jnp.concatenate(
                            [source(d, half, (base + g) * per + j)[panel, f, k] for half in range(2) for j in range(per)], axis=0
                        )
                        for k in range(2)
                        for g in range(groups)
                    ],
                    axis=1,
                )
                real = dot(jnp.concatenate(left[0] + left[1], axis=1), right)
                store(f, 0, real)
                imag = dot(jnp.concatenate(left[1] + [-n for n in left[0]], axis=1), right)
                store(f, 1, imag)


def local(spectra, half_width, panel_block, panel_offset):
    f_dev, parts, ch_dev, windows = spectra.shape
    n_chan, n_band = lax.axis_size("chan"), lax.axis_size("band")
    bins, channels = f_dev * n_band, ch_dev * n_chan
    groups = windows // LANES
    me = lax.axis_index("chan")
    hbm = pl.BlockSpec(memory_space=pl.ANY)
    vmem = pl.BlockSpec(memory_space=pltpu.VMEM)

    ring = list(range(0, n_chan, 2)) + list(range(1, n_chan, 2))[::-1]

    is_me = jnp.broadcast_to((panel_block == me)[:, None, None, None, None], (NPANEL, 1, 1, 1, LANES))
    is_me = is_me.astype(jnp.float32)

    half_rows = ch_dev // 2
    keep_rows = half_rows + HALO
    band = lax.axis_index("band")
    near = band % 2 == 0

    def flip(block, bit):
        return lax.ppermute(block, "band", [(b, b ^ bit) for b in range(n_band)])

    def outward(block):
        pairs = [
            (c * n_band + b, (c + (2 * (b % 2) - 1)) * n_band + (b ^ 1))
            for c in range(n_chan)
            for b in range(n_band)
            if 0 <= c + (2 * (b % 2) - 1) < n_chan
        ]
        return lax.ppermute(block, ("chan", "band"), pairs)

    def power_of(block):
        return jnp.sum(jnp.square(block.astype(jnp.float32)), axis=(0, 1))

    low, high = power_of(spectra[:, :, :HALO]), power_of(spectra[:, :, ch_dev - HALO :])
    edge = jnp.where(near, low, high) + flip(jnp.where(near, high, low), 1)
    power = power_of(spectra)
    first, second = power[:keep_rows], power[half_rows - HALO :]
    share = jnp.where(near, first, second) + flip(jnp.where(near, second, first), 1)
    bit = 2
    while bit * 2 < n_band:
        edge = edge + flip(edge, bit)
        share = share + flip(share, bit)
        bit *= 2
    edge = edge + flip(edge, bit)
    halo = outward(edge)
    spans = spans_of(groups)
    shares = [share[:, base * LANES : (base + n) * LANES] for base, n in spans]
    theirs = []
    for i in range(len(spans)):
        theirs.append(flip(shares[i], bit))
    widths = half_width.reshape(1, windows)

    piece = (NPANEL, f_dev, parts, HALF // SUBS, LANES)
    block = (f_dev, parts, ch_dev, LANES)
    cuts = 2 * SUBS
    normed, own = [], [[], []]
    for i, (base, n_groups) in enumerate(spans):
        span = n_groups * LANES
        scale = pl.pallas_call(
            functools.partial(scale_kernel, channels, bins),
            grid=(n_groups,),
            out_shape=jax.ShapeDtypeStruct((half_rows, span), jnp.float32),
            in_specs=[pl.BlockSpec((keep_rows, LANES), lambda g: (0, g))] * 2
            + [pl.BlockSpec((HALO, LANES), lambda g, base=base: (0, base + g))]
            + [pl.BlockSpec((1, LANES), lambda g, base=base: (0, base + g))],
            out_specs=pl.BlockSpec((half_rows, LANES), lambda g: (0, g)),
            scratch_shapes=[pltpu.VMEM((half_rows + 4 * HALO, LANES), jnp.float32)] * 2,
            compiler_params=pltpu.CompilerParams(vmem_limit_bytes=6 << 20),
            name="scale",
        )
        scale = scale(shares[i], theirs[i], halo, widths)
        norm = pl.pallas_call(
            functools.partial(norm_kernel, n_groups, SUBS),
            out_shape=[pltpu.VMEM(block, jnp.bfloat16)] * n_groups
            + [pltpu.VMEM(piece, jnp.bfloat16)] * (n_groups * cuts),
            in_specs=[pl.BlockSpec(memory_space=pltpu.SMEM)] + [hbm] * 2 + [vmem],
            out_specs=[vmem] * (n_groups * (1 + cuts)),
            scratch_shapes=[
                pltpu.VMEM((ch_dev, span), jnp.float32),
                pltpu.VMEM(block, jnp.float32),
                pltpu.SemaphoreType.DMA((2,)),
            ],
            compiler_params=pltpu.CompilerParams(vmem_limit_bytes=16 << 20),
            name="norm",
        )
        cut = spectra[..., base * LANES : (base + n_groups) * LANES]
        other = flip(scale, 1)
        outs = norm(panel_offset, scale, other, cut)
        normed += outs[:n_groups]
        outs = outs[n_groups:]
        for g in range(n_groups):
            own[0] += outs[g * cuts : g * cuts + SUBS]
            own[1] += outs[g * cuts + SUBS : (g + 1) * cuts]

    n_chunks = groups * SUBS
    single, n_sends, n_steps = plan(n_chan, n_chunks)
    n_ready = early_groups(n_chan, groups) * SUBS + LAG * (n_chan - 2)
    got = [[], []]
    rest = [own[half][c] for c in range(single, n_chunks) for half in range(2)]
    sends = [own[half][:single] + rest for half in range(2)]

    marks = {LAG: [lax.optimization_barrier(is_me), lax.optimization_barrier(is_me + is_me)]}
    for t in range(LAG + 1, n_sends):
        marks[t] = []
        for half in range(2):
            marks[t].append(lax.optimization_barrier(jnp.minimum(marks[t - 1][half], 2.0 - half)))
    for t in range(n_steps):
        for half in range(2):
            value = sends[half][t] if t < n_sends else got[half][t - LAG]
            if LAG <= t < n_sends:
                mask, mine, back = lax.optimization_barrier((marks[t][half], value, got[half][t - LAG]))
                value = jnp.where(mask > 0, mine, back)
            step = 1 if half == 0 else -1
            pairs = [(ring[i], ring[(i + step) % n_chan]) for i in range(n_chan)]
            got[half].append(lax.ppermute(value, "chan", pairs))

    block = (f_dev, parts, ch_dev, PANEL)
    messages = [*own[0], *own[1], *got[0], *got[1]]
    ahead = early_groups(n_chan, groups)
    sums = []
    if ahead:
        early = pl.pallas_call(
            functools.partial(cross_kernel, 0, ahead, n_chan, n_chunks, n_ready, single, None),
            grid=(NPANEL,),
            out_shape=pltpu.VMEM((NPANEL, *block), jnp.float32),
            in_specs=[pl.BlockSpec(memory_space=pltpu.SMEM)] + [vmem] * (ahead + 2 * n_chunks + 2 * n_ready),
            out_specs=vmem,
            compiler_params=pltpu.CompilerParams(vmem_limit_bytes=16 << 20),
            name="early",
        )
        sums = [early(panel_block, *normed[:ahead], *own[0], *own[1], *got[0][:n_ready], *got[1][:n_ready])]
    return pl.pallas_call(
        functools.partial(
            cross_kernel, ahead, groups - ahead, n_chan, n_chunks, n_steps, single, windows ** (-0.5)
        ),
        grid=(NPANEL,),
        out_shape=jax.ShapeDtypeStruct((NPANEL, *block), jnp.bfloat16),
        in_specs=[pl.BlockSpec(memory_space=pltpu.SMEM)] + [vmem] * (groups - ahead + len(messages) + len(sums)),
        out_specs=pl.BlockSpec((1, *block), lambda p: (p, 0, 0, 0, 0)),
        compiler_params=pltpu.CompilerParams(vmem_limit_bytes=20 << 20),
        name="cross",
    )(panel_block, *normed[ahead:], *messages, *sums)


def solution(mesh):
    placed = (P("band", None, "chan", None), P(), P(), P())
    return jax.shard_map(
        local,
        mesh=mesh,
        in_specs=placed,
        out_specs=P(None, "band", None, "chan", None),
        check_vma=False,
    )
```
